768 devices in a mesh: dp: 64 (over z_lo, y, core), chan: 12 (over x, z_hi).
Axes of the slice: x: 4, y: 8, z: 12 (z_hi: 3, z_lo: 4; z = z_hi * 4 + z_lo), core: 2. Of those that a mesh axis runs over, the one named last changes fastest.
Arguments:
- pixels: bfloat16 [6144, 1536], P('dp', 'chan'), may hold values from -6 to 6
- embed_weight: bfloat16 [96, 16, 1024], P('chan'), may hold values from -1.5 to 1.5
- channel_bias: bfloat16 [96, 1024], P('chan'), may hold values from -3 to 3
- agg_query: bfloat16 [12, 1024], P('chan'), may hold values from -0.375 to 0.375
- key_weight: bfloat16 [1024, 768], P(None, 'chan'), may hold values from -0.1875 to 0.1875
- value_weight: bfloat16 [1024, 768], P(None, 'chan'), may hold values from -0.1875 to 0.1875
- final_query: bfloat16 [12, 64], P('chan'), may hold values from -10 to 10
- out_weight: bfloat16 [768, 1024], P('chan'), may hold values from -0.21875 to 0.21875
- group_counts: int32 [12], P('chan'), may hold values from 4 to 8, as said below
- grad_output: bfloat16 [6144, 1024], P('dp'), may hold values from -0.078125 to 0.078125
Outputs:
- layer_out: bfloat16 [6144, 1024], P('dp')
- grad_embed: float32 [96, 16, 1024], P('chan')
- grad_bias: float32 [96, 1024], P('chan')
- grad_agg: float32 [12, 1024], P('chan')
- grad_key: float32 [1024, 768], P(None, 'chan')
- grad_value: float32 [1024, 768], P(None, 'chan')
- grad_query: float32 [12, 64], P('chan')
- grad_out: float32 [768, 1024], P('chan')
The draws below stay inside these ranges and needn't reach their ends.
Inputs may be any that keep to these rules, and one draw needn't show every extreme that they name: A group's first group_counts[g] channels are live; some group has all 8 live.
All inputs are finite; a program needn't handle non-finite values.
Results may differ from the reference program's by a relative error of at most 0.018.
The reference program's roundings to bfloat16 on the way count: a program that leaves them out, or rounds other values in their place, can miss the bound.
Values may be sent and summed in bfloat16 or wider, within the bound.
A program may use at most 32 MiB of HBM per device.

```python
import math
import jax
import jax.numpy as jnp
from jax import lax

D = 1024
PP = 16
CH_DEV = 8
HD = 64
TOK_DEV = 96
GROUPS = 12
HEADS = 12
CHANNELS = 96
TOKENS = 6144
N_DP = 64


def draw_group_counts(key, part):
    first_key, second_key = jax.random.split(jax.random.fold_in(key, 17))
    counts = jax.random.randint(first_key, (GROUPS,), CH_DEV // 2, CH_DEV + 1)
    chosen = jax.random.randint(second_key, (), 0, GROUPS)
    return jnp.where(jnp.arange(GROUPS) == chosen, CH_DEV, counts).astype(jnp.int32)


def shard_levels(key, extent, cuts, low, top_value):
    def one(axis_at, blocks):
        heights = jax.random.uniform(jax.random.fold_in(jax.random.fold_in(key, 6), axis_at), (blocks,), jnp.float32, low / len(cuts), top_value / len(cuts))
        return jnp.repeat(jnp.exp(heights), extent[axis_at] // blocks).reshape((-1,) + (1,) * (len(extent) - axis_at - 1))

    loudness = one(*cuts[0])
    for cut in cuts[1:]:
        loudness = loudness * one(*cut)
    return loudness


def centred(rng, shape, width, most, cuts=(), kind=jnp.bfloat16):
    drawn = jax.random.normal(rng, shape, jnp.float32) * width
    if len(cuts) > 0:
        drawn = shard_levels(rng, shape, cuts, -0.22, 0.18) * drawn
    return jnp.clip(drawn, min=-most, max=most).astype(kind)


def setup_inputs(seed: int = 0) -> dict:
    key_of = jax.random.split(jax.random.key(seed), 11)
    pixels = centred(key_of[0], (TOKENS, CHANNELS * PP), 1.0, 6.0, ((0, 64), (1, 12)))
    embed_weight = centred(key_of[1], (CHANNELS, PP, D), PP ** -0.5, 1.5, ((0, 12),))
    channel_bias = centred(key_of[2], (CHANNELS, D), 0.5, 3.0, ((0, 12),))
    agg_query = centred(key_of[3], (GROUPS, D), (D // 4) ** -0.5, 0.375, ((0, 12),))
    key_weight = centred(key_of[4], (D, HEADS * HD), D ** -0.5, 0.1875, ((1, 12),))
    value_weight = centred(key_of[5], (D, HEADS * HD), D ** -0.5, 0.1875, ((1, 12),))
    final_query = centred(key_of[6], (HEADS, HD), 2.0, 10.0, ((0, 12),))
    out_weight = centred(key_of[7], (HEADS * HD, D), (HEADS * HD) ** -0.5, 0.21875, ((0, 12),))
    group_counts = draw_group_counts(jax.random.fold_in(key_of[10], 71), 0)
    grad_output = centred(key_of[9], (TOKENS, D), TOKENS ** -0.5, 0.078125, ((0, 64),))
    return dict(pixels=pixels, embed_weight=embed_weight, channel_bias=channel_bias, agg_query=agg_query, key_weight=key_weight, value_weight=value_weight, final_query=final_query, out_weight=out_weight, group_counts=group_counts, grad_output=grad_output)


softcap = 15.0

def rounded(value):
    return lax.optimization_barrier(value.astype(jnp.bfloat16)).astype(jnp.float32)

def block_pass(pixel_rows, grad_rows, embed_weight, channel_bias, agg_query, key_weight, value_weight, final_query, out_weight, live_mask):
    tok_rows = pixel_rows.shape[0]
    patches = pixel_rows.reshape(tok_rows, CHANNELS, PP).astype(jnp.float32)
    embed_wide = rounded(jnp.einsum('tcp,cpd->tcd', patches, embed_weight.astype(jnp.float32)) + channel_bias.astype(jnp.float32)[None])
    query_rows = jnp.repeat(agg_query.astype(jnp.float32), CH_DEV, axis=0)
    agg_capped = softcap * jnp.tanh(jnp.einsum('tcd,cd->tc', embed_wide, query_rows) / softcap)
    agg_exp = jnp.exp(agg_capped) * live_mask[None]
    agg_total = agg_exp.reshape(tok_rows, GROUPS, CH_DEV).sum(-1)
    agg_weight = agg_exp / jnp.repeat(agg_total, CH_DEV, axis=1)
    agg_round = rounded(agg_weight)
    embed_four = embed_wide.reshape(tok_rows, GROUPS, CH_DEV, D)
    group_token = rounded(jnp.einsum('tgc,tgcd->tgd', agg_round.reshape(tok_rows, GROUPS, CH_DEV), embed_four))
    key_three = key_weight.astype(jnp.float32).reshape(D, HEADS, HD)
    value_three = value_weight.astype(jnp.float32).reshape(D, HEADS, HD)
    query_heads = final_query.astype(jnp.float32)
    keys = rounded(jnp.einsum('tgd,dhk->tghk', group_token, key_three))
    values = rounded(jnp.einsum('tgd,dhk->tghk', group_token, value_three))
    head_capped = softcap * jnp.tanh(jnp.einsum('tghk,hk->thg', keys, query_heads) / math.sqrt(HD) / softcap)
    head_exp = jnp.exp(head_capped)
    head_prob = head_exp / head_exp.sum(-1, keepdims=True)
    head_round = rounded(head_prob)
    attended = rounded(jnp.einsum('thg,tghk->thk', head_round, values))
    out_three = out_weight.astype(jnp.float32).reshape(HEADS, HD, D)
    layer_rows = jnp.einsum('thk,hkd->td', attended, out_three).astype(jnp.bfloat16)
    grad_wide = grad_rows.astype(jnp.float32)
    grad_out = jnp.einsum('thk,td->hkd', attended, grad_wide).reshape(HEADS * HD, D)
    attended_grad = rounded(jnp.einsum('td,hkd->thk', grad_wide, out_three))
    prob_grad = jnp.einsum('thk,tghk->thg', attended_grad, values)
    value_grad = rounded(jnp.einsum('thg,thk->tghk', head_round, attended_grad))
    score_grad = head_prob * (prob_grad - lax.optimization_barrier(jnp.sum(head_prob * prob_grad, -1, keepdims=True)))
    raw_grad = score_grad * (1.0 - (head_capped / softcap) ** 2) / math.sqrt(HD)
    key_grad = rounded(jnp.einsum('thg,hk->tghk', raw_grad, query_heads))
    grad_query = jnp.einsum('thg,tghk->hk', raw_grad, keys)
    grad_key = jnp.einsum('tgd,tghk->dhk', group_token, key_grad).reshape(D, HEADS * HD)
    grad_value = jnp.einsum('tgd,tghk->dhk', group_token, value_grad).reshape(D, HEADS * HD)
    head_parts = rounded(jnp.einsum('tghk,dhk->tghd', key_grad, key_three) + jnp.einsum('tghk,dhk->tghd', value_grad, value_three))
    token_grad = head_parts.sum(2)
    mix_grad = jnp.einsum('tgd,tgcd->tgc', token_grad, embed_four).reshape(tok_rows, CHANNELS)
    mix_weighted = (agg_weight * mix_grad).reshape(tok_rows, GROUPS, CH_DEV).sum(-1)
    agg_raw_grad = agg_weight * (mix_grad - jnp.repeat(mix_weighted, CH_DEV, axis=1)) * (1.0 - (agg_capped / softcap) ** 2)
    token_rep = jnp.repeat(token_grad, CH_DEV, axis=1)
    embed_grad = rounded(agg_round[..., None] * token_rep + agg_raw_grad[..., None] * query_rows[None])
    grad_agg = jnp.einsum('tc,tcd->cd', agg_raw_grad, embed_wide).reshape(GROUPS, CH_DEV, D).sum(1)
    grad_embed = jnp.einsum('tcp,tcd->cpd', patches, embed_grad)
    grad_bias = embed_grad.sum(0)
    return (layer_rows, (grad_embed, grad_bias, grad_agg, grad_key, grad_value, grad_query, grad_out))

def reference(pixels, embed_weight, channel_bias, agg_query, key_weight, value_weight, final_query, out_weight, group_counts, grad_output):
    live_mask = (jnp.arange(CHANNELS, dtype=jnp.int32) % CH_DEV < jnp.repeat(group_counts, CH_DEV)).astype(jnp.float32)
    pixel_blocks = pixels.reshape(N_DP, TOK_DEV, CHANNELS * PP)
    grad_blocks = grad_output.reshape(N_DP, TOK_DEV, D)
    zeros = (jnp.zeros((CHANNELS, PP, D), jnp.float32), jnp.zeros((CHANNELS, D), jnp.float32), jnp.zeros((GROUPS, D), jnp.float32), jnp.zeros((D, HEADS * HD), jnp.float32), jnp.zeros((D, HEADS * HD), jnp.float32), jnp.zeros((HEADS, HD), jnp.float32), jnp.zeros((HEADS * HD, D), jnp.float32))

    def advance(carry, inputs):
        layer_rows, grads = block_pass(inputs[0], inputs[1], embed_weight, channel_bias, agg_query, key_weight, value_weight, final_query, out_weight, live_mask)
        return (tuple((left + right for left, right in zip(carry, grads))), layer_rows)
    totals, layer = lax.scan(advance, zeros, (pixel_blocks, grad_blocks))
    return (layer.reshape(TOKENS, D), totals[0], totals[1], totals[2], totals[3], totals[4], totals[5], totals[6])
```

```python
import jax
import jax.numpy as jnp
from jax import lax
from jax.experimental import pallas as pl
from jax.experimental.pallas import tpu as pltpu
from jax.sharding import PartitionSpec as P

MESH = pl.DeviceIdType.MESH
NX, NH, NY, NL = 4, 3, 8, 4
CH = NX * NH
TOK, D = 96, 1024
HEADS, HD = 12, 64
PARTS = 3
PR = TOK // PARTS
PH = PR // 2
CAP = 15.0
LANES = 640

f32, bf16 = jnp.float32, jnp.bfloat16


def coords():
    dp, ch = lax.axis_index("dp"), lax.axis_index("chan")
    return dp, ch


def gather_kernel(tok, wp, kt, tok_all, w_all, kt_all, loc, sz, rz, sx, rx, sw, rw, sy, ry, sb, rb):
    dp, ch = coords()
    x, zh = ch // NH, ch % NH
    core, y, zl = dp % 2, (dp // 2) % NY, dp // (2 * NY)
    xn, xp = (x + 1) % NX, (x + NX - 1) % NX
    yn, yp = (y + 1) % NY, (y + NY - 1) % NY

    def at_chan(x_, z_):
        return (dp, x_ * NH + z_)

    def at_dp(y_, c_):
        return (zl * (2 * NY) + y_ * 2 + c_, ch)

    zdev = [at_chan(x, (zh + k + 1) % NH) for k in range(2)]
    xdev = [at_chan(xn, zh), at_chan(xp, zh)]
    ydev = [at_dp(yn, core), at_dp(yp, core)]
    sib = at_dp(y, 1 - core)

    barrier = pltpu.get_barrier_semaphore()
    for dev in zdev + xdev + ydev + [sib]:
        pl.semaphore_signal(barrier, inc=1, device_id=dev, device_id_type=MESH)
    pl.semaphore_wait(barrier, 7)

    started = []

    def send(src, dst, ss, rs, dev):
        copy = pltpu.make_async_remote_copy(
            src_ref=src, dst_ref=dst, send_sem=ss, recv_sem=rs, device_id=dev, device_id_type=MESH
        )
        copy.start()
        started.append(copy)

    def arrive(dst, ss, rs):
        pltpu.make_async_remote_copy(
            src_ref=dst, dst_ref=dst, send_sem=ss, recv_sem=rs, device_id=sib, device_id_type=MESH
        ).wait_recv()

    def owner(dx, k):
        return ((x + NX - dx) % NX) * NH + (zh + NH - k) % NH

    blk = y * 2 + core
    small = [(wp, lambda c: w_all.at[blk, c]), (kt, lambda c: kt_all.at[c])]

    def part(c, p):
        return tok_all.at[c, pl.ds(p * PR, PR)]

    def half(c, p, h):
        return tok_all.at[c, pl.ds(p * PR + h * PH, PH)]

    local = [
        pltpu.make_async_copy(tok, tok_all.at[ch], loc.at[0]),
        pltpu.make_async_copy(wp, w_all.at[blk, ch], loc.at[1]),
        pltpu.make_async_copy(kt, kt_all.at[ch], loc.at[2]),
    ]
    for copy in local:
        copy.start()
    for i, (src, dst) in enumerate(small):
        for k in range(2):
            send(src, dst(ch), sw.at[i, k], rw.at[i, k], zdev[k])
        for d in range(2):
            send(src, dst(ch), sw.at[i, 2 + 3 * d], rw.at[i, 2 + 3 * d], xdev[d])
    for p in range(PARTS):
        mine = tok.at[pl.ds(p * PR, PR)]
        for k in range(2):
            send(mine, part(ch, p), sz.at[k, p], rz.at[k, p], zdev[k])
        for d in range(2):
            send(mine, part(ch, p), sx.at[d, 0, p], rx.at[d, 0, p], xdev[d])
    for copy in local:
        copy.wait()

    for k in (1, 2):
        for i, (_, dst) in enumerate(small):
            c = owner(0, k)
            arrive(dst(c), sw.at[i, k - 1], rw.at[i, k - 1])
            for d in range(2):
                send(dst(c), dst(c), sw.at[i, 2 + 3 * d + k], rw.at[i, 2 + 3 * d + k], xdev[d])
    for k in range(3):
        for i, (_, dst) in enumerate(small):
            c = owner(1, k)
            arrive(dst(c), sw.at[i, 2 + k], rw.at[i, 2 + k])
            send(dst(c), dst(c), sw.at[i, 8 + k], rw.at[i, 8 + k], xdev[0])

    def relay(k, p):
        c = owner(1, k)
        arrive(part(c, p), sx.at[0, k, p], rx.at[0, k, p])
        send(half(c, p, 0), half(c, p, 0), sx.at[2, k, p], rx.at[2, k, p], xdev[0])
        c = owner(NX - 1, k)
        arrive(part(c, p), sx.at[1, k, p], rx.at[1, k, p])
        send(half(c, p, 1), half(c, p, 1), sx.at[3, k, p], rx.at[3, k, p], xdev[1])

    for p in range(PARTS):
        relay(0, p)
    for k in range(3):
        for i, (_, dst) in enumerate(small):
            c = owner(NX - 1, k)
            arrive(dst(c), sw.at[i, 5 + k], rw.at[i, 5 + k])
            c = owner(2, k)
            arrive(dst(c), sw.at[i, 8 + k], rw.at[i, 8 + k])

    def sub(y_, h):
        return w_all.at[((y_ + 2 * NY) % NY) * 2 + core, pl.ds(6 * h, 6)]

    def ystep(s):
        for h in range(2):
            if s < 3 or h == 0:
                send(sub(y - s, h), sub(y - s, h), sy.at[0, s, h], ry.at[0, s, h], ydev[0])
            if s < 3 or h == 1:
                send(sub(y + s, h), sub(y + s, h), sy.at[1, s, h], ry.at[1, s, h], ydev[1])

    def yarrive(s):
        for h in range(2):
            if s < 3 or h == 0:
                arrive(sub(y - 1 - s, h), sy.at[0, s, h], ry.at[0, s, h])
                send(sub(y - 1 - s, h), sub(y - 1 - s, h), sb.at[0, s, h], rb.at[0, s, h], sib)
            if s < 3 or h == 1:
                arrive(sub(y + 1 + s, h), sy.at[1, s, h], ry.at[1, s, h])
                send(sub(y + 1 + s, h), sub(y + 1 + s, h), sb.at[1, s, h], rb.at[1, s, h], sib)
            if s + 1 < 3 or (s + 1 == 3 and h == 0):
                send(sub(y - 1 - s, h), sub(y - 1 - s, h), sy.at[0, s + 1, h], ry.at[0, s + 1, h], ydev[0])
            if s + 1 < 3 or (s + 1 == 3 and h == 1):
                send(sub(y + 1 + s, h), sub(y + 1 + s, h), sy.at[1, s + 1, h], ry.at[1, s + 1, h], ydev[1])

    ystep(0)
    for h in range(2):
        send(sub(y, h), sub(y, h), sb.at[2, 0, h], rb.at[2, 0, h], sib)
    for p in range(PARTS):
        for k in (1, 2):
            c = owner(0, k)
            arrive(part(c, p), sz.at[k - 1, p], rz.at[k - 1, p])
            for d in range(2):
                send(part(c, p), part(c, p), sx.at[d, k, p], rx.at[d, k, p], xdev[d])
        yarrive(p)
        for k in (1, 2):
            relay(k, p)
    yarrive(3)
    for k in range(3):
        for p in range(PARTS):
            c = owner(2, k)
            arrive(half(c, p, 0), sx.at[2, k, p], rx.at[2, k, p])
            arrive(half(c, p, 1), sx.at[3, k, p], rx.at[3, k, p])

    def theirs(y_, h):
        return w_all.at[((y_ + 2 * NY) % NY) * 2 + 1 - core, pl.ds(6 * h, 6)]

    for h in range(2):
        arrive(theirs(y, h), sb.at[2, 0, h], rb.at[2, 0, h])
        for s in range(4):
            if s < 3 or h == 0:
                arrive(theirs(y - 1 - s, h), sb.at[0, s, h], rb.at[0, s, h])
            if s < 3 or h == 1:
                arrive(theirs(y + 1 + s, h), sb.at[1, s, h], rb.at[1, s, h])
    for copy in started:
        copy.wait_send()


def gather_all(tok, wp, kt):
    any_ = pl.BlockSpec(memory_space=pl.ANY)
    vmem = pl.BlockSpec(memory_space=pltpu.VMEM)
    dma = pltpu.SemaphoreType.DMA
    return pl.pallas_call(
        gather_kernel,
        out_shape=(
            jax.ShapeDtypeStruct((CH, TOK, D), bf16),
            jax.ShapeDtypeStruct((2 * NY, CH, 8, D), bf16),
            jax.ShapeDtypeStruct((CH, 16, 128), bf16),
        ),
        in_specs=[vmem, vmem, vmem],
        out_specs=(any_, any_, any_),
        scratch_shapes=[
            dma((3,)),
            dma((2, PARTS)),
            dma((2, PARTS)),
            dma((4, 3, PARTS)),
            dma((4, 3, PARTS)),
            dma((2, 11)),
            dma((2, 11)),
            dma((2, 4, 2)),
            dma((2, 4, 2)),
            dma((3, 4, 2)),
            dma((3, 4, 2)),
        ],
        compiler_params=pltpu.CompilerParams(collective_id=0, has_side_effects=True),
        name="gather_all",
    )(tok, wp, kt)


OWN = NY * NL


def sum_kernel(g, out, half_in, held, mine, acc, s0, r0, s1, r1, s2, r2, s3, r3):
    dp, ch = coords()
    core, own = dp % 2, dp // 2
    sib = (own * 2 + 1 - core, ch)

    barrier = pltpu.get_barrier_semaphore()

    @pl.loop(1, OWN)
    def _(j):
        pl.semaphore_signal(
            barrier, inc=1, device_id=(((own + j) % OWN) * 2 + core, ch), device_id_type=MESH
        )

    pl.semaphore_signal(barrier, inc=1, device_id=sib, device_id_type=MESH)
    pl.semaphore_wait(barrier, OWN)

    def remote(src, dst, ss, rs, dev):
        return pltpu.make_async_remote_copy(
            src_ref=src, dst_ref=dst, send_sem=ss, recv_sem=rs, device_id=dev, device_id_type=MESH
        )

    pair = remote(g.at[1 - core], half_in, s0, r0, sib)
    pair.start()
    pair.wait_recv()
    acc[...] = (g[core].astype(f32) + half_in[...].astype(f32)).astype(bf16)

    @pl.loop(1, OWN)
    def _(j):
        to = (own + j) % OWN
        remote(acc.at[to], held.at[own], s1.at[to], r1.at[own], (to * 2 + core, ch)).start()

    total = acc[own].astype(f32)

    def add(j, total):
        at = (own + OWN - j) % OWN
        remote(acc.at[at], held.at[at], s1.at[at], r1.at[at], sib).wait_recv()
        return total + held[at].astype(f32)

    total = lax.fori_loop(1, OWN, add, total)
    mine[...] = total.astype(bf16)

    @pl.loop(1, OWN)
    def _(j):
        to = (own + j) % OWN
        remote(mine, out.at[core, own], s2.at[to], r2.at[own], (to * 2 + core, ch)).start()

    put = pltpu.make_async_copy(mine, out.at[core, own], s3.at[1])
    put.start()

    @pl.loop(1, OWN)
    def _(j):
        at = (own + OWN - j) % OWN
        remote(mine, out.at[core, at], s2.at[at], r2.at[at], sib).wait_recv()

    put.wait()
    back = remote(out.at[core], out.at[core], s3.at[0], r3, sib)
    back.start()
    remote(out.at[1 - core], out.at[1 - core], s3.at[0], r3, sib).wait_recv()
    back.wait_send()
    pair.wait_send()

    @pl.loop(1, OWN)
    def _(j):
        to = (own + j) % OWN
        remote(acc.at[to], held.at[own], s1.at[to], r1.at[own], sib).wait_send()
        remote(mine, out.at[core, own], s2.at[to], r2.at[own], sib).wait_send()


def sum_over_dp(g):
    vmem = pl.BlockSpec(memory_space=pltpu.VMEM)
    dma = pltpu.SemaphoreType.DMA
    shape = (OWN, 8, LANES)
    return pl.pallas_call(
        sum_kernel,
        out_shape=jax.ShapeDtypeStruct((2, *shape), bf16),
        in_specs=[vmem],
        out_specs=vmem,
        scratch_shapes=[
            pltpu.VMEM(shape, bf16),
            pltpu.VMEM(shape, bf16),
            pltpu.VMEM(shape[1:], bf16),
            pltpu.VMEM(shape, bf16),
            dma,
            dma,
            dma((OWN,)),
            dma((OWN,)),
            dma((OWN,)),
            dma((OWN,)),
            dma((2,)),
            dma,
        ],
        compiler_params=pltpu.CompilerParams(collective_id=1, has_side_effects=True),
        name="sum_over_dp",
    )(g)


def split(value):
    high = lax.reduce_precision(value, 8, 7)
    return high.astype(bf16), (value - high).astype(bf16)


def dot(a, b, ca, cb):
    return lax.dot_general(a, b, (((ca,), (cb,)), ((), ())), preferred_element_type=f32)


def per_device(
    pixels,
    embed_weight,
    channel_bias,
    agg_query,
    key_weight,
    value_weight,
    final_query,
    out_weight,
    group_counts,
    grad_output,
):
    dp, ch = coords()
    channels, pixel_count = embed_weight.shape[:2]
    query_row = agg_query[0]
    query_head = final_query[0].astype(f32)

    patches = pixels.reshape(TOK, channels, pixel_count)
    embedded = (
        jnp.einsum("tcp,cpd->tcd", patches, embed_weight, preferred_element_type=f32)
        + channel_bias.astype(f32)[None]
    ).astype(bf16)
    live_mask = (jnp.arange(channels, dtype=jnp.int32) < group_counts[0]).astype(f32)
    agg_capped = CAP * jnp.tanh(
        jnp.einsum("tcd,d->tc", embedded, query_row, preferred_element_type=f32) / CAP
    )
    agg_exp = jnp.exp(agg_capped) * live_mask[None]
    agg_weight = agg_exp / jnp.sum(agg_exp, -1, keepdims=True)
    agg_round = agg_weight.astype(bf16)
    group_token = jnp.einsum(
        "tc,tcd->td", agg_round, embedded, preferred_element_type=f32
    ).astype(bf16)

    key_query = jnp.sum(key_weight.astype(f32) * query_head[None], 1)
    kq_high, kq_low = split(key_query)
    kt = jnp.concatenate([kq_high.reshape(8, 128), kq_low.reshape(8, 128)], 0)
    shard = jnp.concatenate([value_weight.T, out_weight], 0)
    piece = lax.dynamic_slice_in_dim(shard, (dp % 16) * 8, 8, 0)
    tokens, weights, kts = gather_all(group_token, piece, kt)
    flat = tokens.reshape(CH * TOK, D)
    all_value = weights[:NY].reshape(HEADS * HD, D)
    all_out = weights[NY:].reshape(HEADS * HD, D)
    kts = kts.reshape(HEADS, 2, D)
    kt_high, kt_low = kts[:, 0], kts[:, 1]

    column_head = (jnp.arange(HEADS * HD) // 8) % HEADS
    expand = (column_head[None] == jnp.arange(HEADS)[:, None]).astype(bf16)
    scores = dot(flat, jnp.concatenate([kt_high, kt_low], 0), 1, 1)
    scores = (scores[:, :HEADS] + scores[:, HEADS:]).reshape(CH, TOK, HEADS)
    tanh = jnp.tanh(scores / 8.0 / CAP)
    head_exp = jnp.exp(CAP * tanh)
    head_prob = head_exp / jnp.sum(head_exp, 0, keepdims=True)
    head_round = head_prob.astype(bf16)
    values = dot(flat, all_value, 1, 1).astype(bf16)
    spread = dot(head_round.reshape(CH * TOK, HEADS), expand, 1, 0)
    attended = jnp.sum((spread * values.astype(f32)).reshape(CH, TOK, HEADS * HD), 0).astype(bf16)
    layer_out = dot(attended, all_out, 1, 0).astype(bf16)
    attended_grad = dot(grad_output, all_out, 1, 1).astype(bf16)
    product = values.reshape(CH, TOK, HEADS * HD).astype(f32) * attended_grad.astype(f32)[None]
    high, low = split(product.reshape(CH * TOK, HEADS * HD))
    prob_grad = (dot(high, expand, 1, 1) + dot(low, expand, 1, 1)).reshape(CH, TOK, HEADS)
    score_grad = head_prob * (prob_grad - jnp.sum(head_prob * prob_grad, 0, keepdims=True))
    raw_grad = score_grad * (1.0 - tanh**2) / 8.0

    my_round = lax.dynamic_index_in_dim(head_round, ch, 2, False)
    my_raw = lax.dynamic_index_in_dim(raw_grad, ch, 2, False)
    my_values = dot(flat, value_weight, 1, 0).astype(bf16).reshape(CH, TOK, HD)
    my_attended = jnp.sum(my_round.astype(f32)[..., None] * my_values.astype(f32), 0).astype(bf16)
    my_grad = dot(grad_output, out_weight, 1, 1).astype(bf16)
    grad_out = dot(my_attended, grad_output, 0, 0)
    value_grad = (my_round.astype(f32)[..., None] * my_grad.astype(f32)[None]).astype(bf16)
    raw_high, raw_low = split(my_raw.reshape(CH * TOK, 1))
    left = jnp.concatenate([value_grad.reshape(CH * TOK, HD), raw_high, raw_low], 1)
    of_tokens = dot(left, flat, 0, 0)

    group_raw = lax.dynamic_index_in_dim(raw_grad, ch, 0, False)
    group_spread = lax.dynamic_slice_in_dim(spread, ch * TOK, TOK, 0)
    group_high, group_low = split(group_raw)
    group_value = (group_spread * attended_grad.astype(f32)).astype(bf16)
    token_grad = dot(group_value, all_value, 1, 0) + dot(
        jnp.concatenate([group_high, group_low, group_high], 1),
        jnp.concatenate([kt_high, kt_high, kt_low], 0),
        1,
        0,
    )
    mix_grad = jnp.einsum("td,tcd->tc", token_grad, embedded.astype(f32))
    mix_weighted = jnp.sum(agg_weight * mix_grad, -1, keepdims=True)
    agg_raw_grad = agg_weight * (mix_grad - mix_weighted) * (1.0 - (agg_capped / CAP) ** 2)
    embed_grad = (
        agg_round.astype(f32)[:, :, None] * token_grad[:, None, :]
        + agg_raw_grad[:, :, None] * query_row.astype(f32)[None, None, :]
    ).astype(bf16)
    grad_agg = jnp.einsum("tc,tcd->d", agg_raw_grad, embedded.astype(f32))[None]
    grad_embed = jnp.einsum("tcp,tcd->cpd", patches, embed_grad, preferred_element_type=f32)
    grad_bias = jnp.sum(embed_grad.astype(f32), 0)

    large = jnp.concatenate(
        [grad_embed.reshape(channels * pixel_count, D), of_tokens[:HD], grad_out], 0
    ).reshape(OWN, 8, D)
    u_row = (of_tokens[HD] + of_tokens[HD + 1])[None]
    few = jnp.concatenate([grad_bias, grad_agg, u_row], 0).reshape(80, 128)
    few = jnp.pad(few, ((0, OWN * 8 - 80), (0, 0))).reshape(OWN, 8, 128)
    packed = jnp.stack(
        [
            jnp.concatenate([large[:, :, :512], few], 2),
            jnp.concatenate([large[:, :, 512:], jnp.zeros_like(few)], 2),
        ]
    ).astype(bf16)
    summed = sum_over_dp(packed).astype(f32)
    large = jnp.concatenate([summed[0, :, :, :512], summed[1, :, :, :512]], 2).reshape(OWN * 8, D)
    few = summed[0, :, :, 512:].reshape(OWN * 8, 128)[:80].reshape(10, D)
    u_row = few[9]
    grad_key = u_row[:, None] * query_head[None]
    grad_query = jnp.sum(u_row[:, None] * key_weight.astype(f32), 0)[None]
    return (
        layer_out,
        large[:128].reshape(channels, pixel_count, D),
        few[:8],
        few[8:9],
        grad_key,
        large[128:192].T,
        grad_query,
        large[192:],
    )


def solution(mesh):
    in_specs = (
        P("dp", "chan"),
        P("chan", None, None),
        P("chan", None),
        P("chan", None),
        P(None, "chan"),
        P(None, "chan"),
        P("chan", None),
        P("chan", None),
        P("chan"),
        P("dp", None),
    )
    out_specs = (
        P("dp", None),
        P("chan", None, None),
        P("chan", None),
        P("chan", None),
        P(None, "chan"),
        P(None, "chan"),
        P("chan", None),
        P("chan", None),
    )
    return jax.shard_map(
        per_device, mesh=mesh, in_specs=in_specs, out_specs=out_specs, check_vma=False
    )
```

```python
import jax
import jax.numpy as jnp
from jax import lax
from jax.experimental import pallas as pl
from jax.experimental.pallas import tpu as pltpu
from jax.sharding import PartitionSpec as P

MESH = pl.DeviceIdType.MESH
NX, NH, NY, NL = 4, 3, 8, 4
CH = NX * NH
TOK, D = 96, 1024
HEADS, HD = 12, 64
WIDE = HEADS * HD
CHANNELS, PP = 8, 16
PARTS = 3
PR = TOK // PARTS
PH = PR // 2
CAP = 15.0
LANES = 640
OWN = NY * NL

f32, bf16 = jnp.float32, jnp.bfloat16


def dot(a, b, ca, cb):
    return lax.dot_general(a, b, (((ca,), (cb,)), ((), ())), preferred_element_type=f32)


def iota(shape, dim):
    return lax.broadcasted_iota(jnp.int32, shape, dim)


def split(value):
    high = value.astype(bf16)
    return high, (value - high.astype(f32)).astype(bf16)


def stacked(row):
    at = iota((8, 128), 0)
    out = jnp.zeros((8, 128), f32)
    for j in range(8):
        out = jnp.where(at == j, row[:, 128 * j : 128 * j + 128], out)
    return out


def step_kernel(
    pix,
    wemb,
    bias,
    aggq,
    kw,
    vw,
    fq,
    outw,
    counts,
    go,
    layer,
    out,
    emb,
    tok_all,
    w_all,
    kt_all,
    tok,
    wp,
    kt,
    head_v,
    head_o,
    kq,
    val,
    left,
    th_s,
    hp_s,
    pg_s,
    g,
    half_in,
    held,
    mine,
    acc,
    sz,
    rz,
    sx,
    rx,
    sw,
    rw,
    sy,
    ry,
    sb,
    rb,
    s0,
    r0,
    s1,
    r1,
    s2,
    r2,
    s3,
    r3,
    s4,
):
    dp, ch = lax.axis_index("dp"), lax.axis_index("chan")
    x, zh = ch // NH, ch % NH
    core, own = dp % 2, dp // 2
    y, zl = own % NY, own // NY
    xn, xp = (x + 1) % NX, (x + NX - 1) % NX
    yn, yp = (y + 1) % NY, (y + NY - 1) % NY

    def at_chan(x_, z_):
        return (dp, x_ * NH + z_)

    def at_dp(y_, c_):
        return (zl * (2 * NY) + y_ * 2 + c_, ch)

    zdev = [at_chan(x, (zh + k + 1) % NH) for k in range(2)]
    xdev = [at_chan(xn, zh), at_chan(xp, zh)]
    ydev = [at_dp(yn, core), at_dp(yp, core)]
    sib = at_dp(y, 1 - core)

    barrier = pltpu.get_barrier_semaphore()
    for dev in zdev + xdev + [sib]:
        pl.semaphore_signal(barrier, inc=1, device_id=dev, device_id_type=MESH)

    @pl.loop(1, OWN)
    def _(j):
        pl.semaphore_signal(
            barrier, inc=1, device_id=(((own + j) % OWN) * 2 + core, ch), device_id_type=MESH
        )

    lane = iota((TOK, 128), 1)
    pixels = pix[...]
    query = aggq[...].astype(f32)
    score = jnp.zeros((TOK, 128), f32)
    for c in range(CHANNELS):
        masked = jnp.where((lane >= PP * c) & (lane < PP * (c + 1)), pixels, jnp.zeros_like(pixels))
        e = (dot(masked, wemb[...], 1, 0) + bias[c : c + 1, :].astype(f32)).astype(bf16)
        emb[c] = e
        s = jnp.sum(e.astype(f32) * query, 1, keepdims=True)
        score = jnp.where(lane == c, s, score)
    capped = CAP * jnp.tanh(score / CAP)
    agg_exp = jnp.exp(capped) * jnp.where(lane < counts[...], 1.0, 0.0)
    agg_weight = agg_exp / jnp.sum(agg_exp, 1, keepdims=True)
    agg_round = agg_weight.astype(bf16).astype(f32)
    token = jnp.zeros((TOK, D), f32)
    for c in range(CHANNELS):
        token += agg_round[:, c : c + 1] * emb[c].astype(f32)
    tok[...] = token.astype(bf16)
    tok_all[pl.ds(pl.multiple_of(ch * TOK, 32), TOK), :] = tok[...]

    eye = (iota((128, 128), 0) == iota((128, 128), 1)).astype(f32).astype(bf16)
    flipped = dot(eye[:HD, :HD], vw[...], 1, 1)
    head_v[:HD] = flipped.astype(bf16)
    head_v[HD:] = jnp.zeros((HD, D), bf16)
    head_o[:HD] = outw[...]
    head_o[HD:] = jnp.zeros((HD, D), bf16)
    for q in range(4):
        wp[q] = head_v[16 * q : 16 * q + 16, :]
        wp[4 + q] = outw[16 * q : 16 * q + 16, :]
    fq8 = jnp.broadcast_to(fq[...].astype(f32), (16, HD)).astype(bf16)
    kt[...] = stacked(dot(fq8, kw[...], 1, 1)[:1])
    kt_all[ch] = kt[...]

    started = []

    def remote(src, dst, ss, rs, dev):
        return pltpu.make_async_remote_copy(
            src_ref=src, dst_ref=dst, send_sem=ss, recv_sem=rs, device_id=dev, device_id_type=MESH
        )

    def send(src, dst, ss, rs, dev):
        copy = remote(src, dst, ss, rs, dev)
        copy.start()
        started.append(copy)

    def arrive(dst, ss, rs):
        remote(dst, dst, ss, rs, sib).wait_recv()

    def owner(dx, k):
        return ((x + NX - dx) % NX) * NH + (zh + NH - k) % NH

    def at_rows(c, start, rows):
        return tok_all.at[pl.ds(pl.multiple_of(c * TOK + start, 16), rows)]

    lanes = pl.multiple_of(core * 512, 512)
    wmine = wp.at[y, :, pl.ds(lanes, 512)]

    def piece(c):
        return w_all.at[pl.ds(pl.multiple_of((y * CH + c) * 16, 16), 16), pl.ds(lanes, 512)]

    small = [(wmine, piece), (kt, lambda c: kt_all.at[c])]

    def part(c, p):
        return at_rows(c, p * PR, PR)

    def half(c, p, h):
        return at_rows(c, p * PR + h * PH, PH)

    place = pltpu.make_async_copy(wmine, piece(ch), s4)
    place.start()
    pl.semaphore_wait(barrier, OWN + 4)

    for i, (src, dst) in enumerate(small):
        for k in range(2):
            send(src, dst(ch), sw.at[i, k], rw.at[i, k], zdev[k])
        for d in range(2):
            send(src, dst(ch), sw.at[i, 2 + 3 * d], rw.at[i, 2 + 3 * d], xdev[d])
    for p in range(PARTS):
        own_part = tok.at[pl.ds(p * PR, PR)]
        for k in range(2):
            send(own_part, part(ch, p), sz.at[k, p], rz.at[k, p], zdev[k])
        for d in range(2):
            send(own_part, part(ch, p), sx.at[d, 0, p], rx.at[d, 0, p], xdev[d])

    place.wait()

    for k in (1, 2):
        for i, (_, dst) in enumerate(small):
            c = owner(0, k)
            arrive(dst(c), sw.at[i, k - 1], rw.at[i, k - 1])
            for d in range(2):
                send(dst(c), dst(c), sw.at[i, 2 + 3 * d + k], rw.at[i, 2 + 3 * d + k], xdev[d])
    for k in range(3):
        for i, (_, dst) in enumerate(small):
            c = owner(1, k)
            arrive(dst(c), sw.at[i, 2 + k], rw.at[i, 2 + k])
            send(dst(c), dst(c), sw.at[i, 8 + k], rw.at[i, 8 + k], xdev[0])

    def relay(k, p):
        c = owner(1, k)
        arrive(part(c, p), sx.at[0, k, p], rx.at[0, k, p])
        send(half(c, p, 0), half(c, p, 0), sx.at[2, k, p], rx.at[2, k, p], xdev[0])
        c = owner(NX - 1, k)
        arrive(part(c, p), sx.at[1, k, p], rx.at[1, k, p])
        send(half(c, p, 1), half(c, p, 1), sx.at[3, k, p], rx.at[3, k, p], xdev[1])

    for p in range(PARTS):
        relay(0, p)
    for k in range(3):
        for i, (_, dst) in enumerate(small):
            c = owner(NX - 1, k)
            arrive(dst(c), sw.at[i, 5 + k], rw.at[i, 5 + k])
            c = owner(2, k)
            arrive(dst(c), sw.at[i, 8 + k], rw.at[i, 8 + k])

    def rows_of(y_, h, core_):
        at = ((y_ + 2 * NY) % NY) * (CH * 16) + h * 96
        return w_all.at[
            pl.ds(pl.multiple_of(at, 32), 96), pl.ds(pl.multiple_of(core_ * 512, 512), 512)
        ]

    def sub(y_, h):
        return rows_of(y_, h, core)

    def ysend(s, h, d):
        block = sub(y - s, h) if d == 0 else sub(y + s, h)
        send(block, block, sy.at[d, s, h], ry.at[d, s, h], ydev[d])

    def yarrive(s):
        for h in range(2):
            for d in range(2):
                if s < 3 or h == d:
                    block = sub(y - 1 - s, h) if d == 0 else sub(y + 1 + s, h)
                    arrive(block, sy.at[d, s, h], ry.at[d, s, h])
                    if s + 1 < 3 or (s + 1 == 3 and h == d):
                        ysend(s + 1, h, d)
                    send(block, block, sb.at[d, s, h], rb.at[d, s, h], sib)

    for h in range(2):
        for d in range(2):
            ysend(0, h, d)
        send(sub(y, h), sub(y, h), sb.at[2, 0, h], rb.at[2, 0, h], sib)
    for p in range(PARTS):
        for k in (1, 2):
            c = owner(0, k)
            arrive(part(c, p), sz.at[k - 1, p], rz.at[k - 1, p])
            for d in range(2):
                send(part(c, p), part(c, p), sx.at[d, k, p], rx.at[d, k, p], xdev[d])
        yarrive(p)
        for k in (1, 2):
            relay(k, p)
    yarrive(3)
    for k in range(3):
        for p in range(PARTS):
            c = owner(2, k)
            arrive(half(c, p, 0), sx.at[2, k, p], rx.at[2, k, p])
            arrive(half(c, p, 1), sx.at[3, k, p], rx.at[3, k, p])
    for h in range(2):
        arrive(rows_of(y, h, 1 - core), sb.at[2, 0, h], rb.at[2, 0, h])
        for s in range(4):
            for d in range(2):
                if s < 3 or h == d:
                    y_ = y - 1 - s if d == 0 else y + 1 + s
                    arrive(rows_of(y_, h, 1 - core), sb.at[d, s, h], rb.at[d, s, h])
    for copy in started:
        copy.wait_send()

    def fold(at):
        return at - 192 * sum((at >= 192 * n).astype(jnp.int32) for n in (1, 2, 3))

    col, row = fold(iota((128, WIDE), 1)), iota((128, WIDE), 0)
    expand = jnp.where((col >= 16 * row) & (col < 16 * row + 16), 1.0, 0.0).astype(bf16)
    row, col = fold(iota((WIDE, 128), 0)), iota((WIDE, 128), 1)
    gather = jnp.where((row >= 16 * col) & (row < 16 * col + 16), 1.0, 0.0).astype(bf16)
    at = iota((128, 128), 0)
    for j in range(8):
        rows = jnp.zeros((128, 128), f32)
        for h in range(HEADS):
            rows = jnp.where(at == h, kt_all[h, j : j + 1, :], rows)
        high, low = split(rows)
        kq[0, :, 128 * j : 128 * j + 128] = high
        kq[1, :, 128 * j : 128 * j + 128] = low

    grads = go[...]
    all_grad = dot(grads, w_all[WIDE:, :], 1, 1).astype(bf16).astype(f32)
    my_grad = dot(grads, head_o[...], 1, 1).astype(bf16).astype(f32)

    def rows_at(i):
        return pl.ds(pl.multiple_of(i * TOK, 32), TOK)

    def first(i, total):
        t = tok_all[rows_at(i), :]
        v = dot(t, w_all[:WIDE, :], 1, 1).astype(bf16)
        val[rows_at(i), :] = v
        s = dot(t, kq[0], 1, 1) + dot(t, kq[1], 1, 1)
        th = jnp.tanh(s / 8.0 / CAP)
        ex = jnp.exp(CAP * th)
        th_s[i] = th
        hp_s[i] = ex
        high, low = split(v.astype(f32) * all_grad)
        pg_s[i] = dot(high, gather, 1, 0) + dot(low, gather, 1, 0)
        return total + ex

    total = lax.fori_loop(0, CH, first, jnp.zeros((TOK, 128), f32))

    def second(i, carry):
        attended, mean = carry
        hp = hp_s[i] / total
        hp_s[i] = hp
        wide = dot(hp.astype(bf16), expand, 1, 0)
        return attended + wide * val[rows_at(i), :].astype(f32), mean + hp * pg_s[i]

    attended, mean = lax.fori_loop(
        0, CH, second, (jnp.zeros((TOK, WIDE), f32), jnp.zeros((TOK, 128), f32))
    )
    layer[...] = dot(attended.astype(bf16), w_all[WIDE:, :], 1, 0).astype(bf16)

    mine_only = lane == ch

    def third(i, my_attended):
        hp, th = hp_s[i], th_s[i]
        raw = hp * (pg_s[i] - mean) * (1.0 - th * th) / 8.0
        pg_s[i] = raw
        weight = jnp.sum(
            jnp.where(mine_only, hp.astype(bf16).astype(f32), 0.0), 1, keepdims=True
        )
        high, low = split(jnp.sum(jnp.where(mine_only, raw, 0.0), 1, keepdims=True))
        rows = weight * my_grad
        rows = jnp.where(lane == HD, high.astype(f32), rows)
        rows = jnp.where(lane == HD + 1, low.astype(f32), rows)
        left[rows_at(i), :] = rows.astype(bf16)
        v = dot(tok_all[rows_at(i), :], head_v[...], 1, 1).astype(bf16)
        return my_attended + weight * v.astype(f32)

    my_attended = lax.fori_loop(0, CH, third, jnp.zeros((TOK, 128), f32))

    hp, raw = hp_s[ch], pg_s[ch]
    wide = dot(hp.astype(bf16), expand, 1, 0)
    high, low = split(raw)
    token_grad = (
        dot((wide * all_grad).astype(bf16), w_all[:WIDE, :], 1, 0)
        + dot(high, kq[0], 1, 0)
        + dot(high, kq[1], 1, 0)
        + dot(low, kq[0], 1, 0)
    )
    mix = jnp.zeros((TOK, 128), f32)
    for c in range(CHANNELS):
        s = jnp.sum(token_grad * emb[c].astype(f32), 1, keepdims=True)
        mix = jnp.where(lane == c, s, mix)
    agg_raw = (
        agg_weight
        * (mix - jnp.sum(agg_weight * mix, 1, keepdims=True))
        * (1.0 - (capped / CAP) * (capped / CAP))
    )

    def put(i, rows):
        for c in range(2):
            g[c, i, :, :512] = rows[:, 512 * c : 512 * c + 512].astype(bf16)

    for i in range(OWN):
        g[0, i, :, 512:] = jnp.zeros((8, 128), bf16)
        g[1, i, :, 512:] = jnp.zeros((8, 128), bf16)

    def put_small(i, row):
        g[0, i, :, 512:] = stacked(row).astype(bf16)

    upright = dot(eye, pixels, 1, 1)
    one = jnp.where(iota((16, TOK), 0) == 0, 1.0, 0.0)
    grad_agg = jnp.zeros((TOK, D), f32)
    for c in range(CHANNELS):
        e = (agg_round[:, c : c + 1] * token_grad + agg_raw[:, c : c + 1] * query).astype(bf16)
        grad_agg += agg_raw[:, c : c + 1] * emb[c].astype(f32)
        rows = jnp.concatenate([upright[PP * c : PP * c + PP], one], 0).astype(bf16)
        res = dot(rows, e, 1, 0)
        put(2 * c, res[:8])
        put(2 * c + 1, res[8:16])
        put_small(c, res[16:17])
    put_small(8, jnp.sum(grad_agg, 0, keepdims=True))

    of_tokens = dot(left[...], tok_all[...], 0, 0)
    of_grads = dot(my_attended.astype(bf16), grads, 0, 0)
    for i in range(8):
        put(16 + i, of_tokens[8 * i : 8 * i + 8])
        put(24 + i, of_grads[8 * i : 8 * i + 8])
    put_small(9, of_tokens[HD : HD + 1] + of_tokens[HD + 1 : HD + 2])

    pair = remote(g.at[1 - core], half_in, s0, r0, sib)
    pair.start()
    pair.wait_recv()
    acc[...] = (g[core].astype(f32) + half_in[...].astype(f32)).astype(bf16)

    @pl.loop(1, OWN)
    def _(j):
        to = (own + j) % OWN
        remote(acc.at[to], held.at[own], s1.at[to], r1.at[own], (to * 2 + core, ch)).start()

    def add(j, total):
        at = (own + OWN - j) % OWN
        remote(acc.at[at], held.at[at], s1.at[at], r1.at[at], sib).wait_recv()
        return total + held[at].astype(f32)

    mine[...] = lax.fori_loop(1, OWN, add, acc[own].astype(f32)).astype(bf16)

    @pl.loop(1, OWN)
    def _(j):
        to = (own + j) % OWN
        remote(mine, out.at[core, own], s2.at[to], r2.at[own], (to * 2 + core, ch)).start()

    out[core, own] = mine[...]

    @pl.loop(1, OWN)
    def _(j):
        at = (own + OWN - j) % OWN
        remote(mine, out.at[core, at], s2.at[at], r2.at[at], sib).wait_recv()

    back = remote(out.at[core], out.at[core], s3, r3, sib)
    back.start()
    remote(out.at[1 - core], out.at[1 - core], s3, r3, sib).wait_recv()
    back.wait_send()
    pair.wait_send()

    @pl.loop(1, OWN)
    def _(j):
        to = (own + j) % OWN
        remote(acc.at[to], held.at[own], s1.at[to], r1.at[own], sib).wait_send()
        remote(mine, out.at[core, own], s2.at[to], r2.at[own], sib).wait_send()


def step(*args):
    vmem = pl.BlockSpec(memory_space=pltpu.VMEM)
    dma = pltpu.SemaphoreType.DMA
    shape = (OWN, 8, LANES)
    return pl.pallas_call(
        step_kernel,
        out_shape=(
            jax.ShapeDtypeStruct((TOK, D), bf16),
            jax.ShapeDtypeStruct((2, *shape), bf16),
        ),
        in_specs=[vmem] * len(args),
        out_specs=(vmem, vmem),
        scratch_shapes=[
            pltpu.VMEM((CHANNELS, TOK, D), bf16),
            pltpu.VMEM((CH * TOK, D), bf16),
            pltpu.VMEM((NY * CH * 16, D), bf16),
            pltpu.VMEM((CH, 8, 128), f32),
            pltpu.VMEM((TOK, D), bf16),
            pltpu.VMEM((NY, 16, D), bf16),
            pltpu.VMEM((8, 128), f32),
            pltpu.VMEM((128, D), bf16),
            pltpu.VMEM((128, D), bf16),
            pltpu.VMEM((2, 128, D), bf16),
            pltpu.VMEM((CH * TOK, WIDE), bf16),
            pltpu.VMEM((CH * TOK, 128), bf16),
            pltpu.VMEM((CH, TOK, 128), f32),
            pltpu.VMEM((CH, TOK, 128), f32),
            pltpu.VMEM((CH, TOK, 128), f32),
            pltpu.VMEM((2, *shape), bf16),
            pltpu.VMEM(shape, bf16),
            pltpu.VMEM(shape, bf16),
            pltpu.VMEM(shape[1:], bf16),
            pltpu.VMEM(shape, bf16),
            dma((2, PARTS)),
            dma((2, PARTS)),
            dma((4, 3, PARTS)),
            dma((4, 3, PARTS)),
            dma((2, 11)),
            dma((2, 11)),
            dma((2, 4, 2)),
            dma((2, 4, 2)),
            dma((3, 4, 2)),
            dma((3, 4, 2)),
            dma,
            dma,
            dma((OWN,)),
            dma((OWN,)),
            dma((OWN,)),
            dma((OWN,)),
            dma,
            dma,
            dma,
        ],
        compiler_params=pltpu.CompilerParams(collective_id=0, has_side_effects=True),
        name="step",
    )(*args)


def finish_kernel(g, fq, kw, embed, bias, agg, key, value, query, outg):
    eye = (iota((HD, HD), 0) == iota((HD, HD), 1)).astype(f32).astype(bf16)

    def rows(i):
        return jnp.concatenate([g[0, i, :, :512], g[1, i, :, :512]], 1)

    def row(i):
        block = g[0, i, :, 512:].astype(f32)
        return jnp.concatenate([block[j : j + 1] for j in range(8)], 1)

    for i in range(16):
        embed[8 * i : 8 * i + 8, :] = rows(i).astype(f32)
    for i in range(8):
        bias[i : i + 1, :] = row(i)
        outg[8 * i : 8 * i + 8, :] = rows(24 + i).astype(f32)
        value_rows = rows(16 + i).astype(f32).astype(bf16)
        part = dot(value_rows, eye[8 * i : 8 * i + 8], 0, 0)
        total = part if i == 0 else total + part
    value[...] = total
    agg[...] = row(8)
    u = row(9)
    u_rows = jnp.broadcast_to(u, (16, D)).astype(bf16)
    only = jnp.where(iota((16, HD), 0) == 0, fq[...].astype(f32), 0.0).astype(bf16)
    key[...] = dot(u_rows, only, 0, 0)
    query[...] = dot(u_rows, kw[...], 1, 0)[:1]


def finish(summed, final_query, key_weight):
    vmem = pl.BlockSpec(memory_space=pltpu.VMEM)

    def shape(*dims):
        return jax.ShapeDtypeStruct(dims, f32)

    return pl.pallas_call(
        finish_kernel,
        out_shape=(
            shape(CHANNELS * PP, D),
            shape(CHANNELS, D),
            shape(1, D),
            shape(D, HD),
            shape(D, HD),
            shape(1, HD),
            shape(HD, D),
        ),
        in_specs=[vmem] * 3,
        out_specs=(vmem,) * 7,
        name="finish",
    )(summed, final_query, key_weight)


def per_device(
    pixels,
    embed_weight,
    channel_bias,
    agg_query,
    key_weight,
    value_weight,
    final_query,
    out_weight,
    group_counts,
    grad_output,
):
    layer_out, summed = step(
        pixels,
        embed_weight.reshape(CHANNELS * PP, D),
        channel_bias,
        agg_query,
        key_weight,
        value_weight,
        final_query,
        out_weight,
        group_counts.reshape(1, 1),
        grad_output,
    )
    embed, bias, agg, key, value, query, outg = finish(summed, final_query, key_weight)
    return layer_out, embed.reshape(CHANNELS, PP, D), bias, agg, key, value, query, outg


def solution(mesh):
    in_specs = (
        P("dp", "chan"),
        P("chan", None, None),
        P("chan", None),
        P("chan", None),
        P(None, "chan"),
        P(None, "chan"),
        P("chan", None),
        P("chan", None),
        P("chan"),
        P("dp", None),
    )
    out_specs = (
        P("dp", None),
        P("chan", None, None),
        P("chan", None),
        P("chan", None),
        P(None, "chan"),
        P(None, "chan"),
        P("chan", None),
        P("chan", None),
    )
    return jax.shard_map(
        per_device, mesh=mesh, in_specs=in_specs, out_specs=out_specs, check_vma=False
    )
```

```python
import jax
import jax.numpy as jnp
from jax import lax
from jax.experimental import pallas as pl
from jax.experimental.pallas import tpu as pltpu
from jax.sharding import PartitionSpec as P

MESH = pl.DeviceIdType.MESH
NX, NH, NY, NL = 4, 3, 8, 4
CH = NX * NH
TOK, D = 96, 1024
HEADS, HD = 12, 64
WIDE = HEADS * HD
CHANNELS, PP = 8, 16
PARTS = 3
PR = TOK // PARTS
PH = PR // 2
CAP = 15.0
OWN = NY * NL
FEW = 5
BATCH = 4
ROWS = BATCH * TOK

f32, bf16 = jnp.float32, jnp.bfloat16


def dot(a, b, ca, cb):
    return lax.dot_general(a, b, (((ca,), (cb,)), ((), ())), preferred_element_type=f32)


def iota(shape, dim):
    return lax.broadcasted_iota(jnp.int32, shape, dim)


def split(value):
    high = value.astype(bf16)
    return high, (value - high.astype(f32)).astype(bf16)


def stacked(row):
    at = iota((8, 128), 0)
    out = jnp.zeros((8, 128), f32)
    for j in range(8):
        out = jnp.where(at == j, row[:, 128 * j : 128 * j + 128], out)
    return out


def step_kernel(
    pix,
    wemb,
    bias,
    aggq,
    kw,
    vw,
    fq,
    outw,
    counts,
    go,
    layer,
    out_a,
    out_b,
    out_c,
    emb,
    tok_all,
    w_all,
    kt_all,
    tok,
    wp,
    kt,
    head_o,
    kq,
    val,
    left,
    th_s,
    hp_s,
    pg_s,
    mv_s,
    g_a,
    g_b,
    g_c,
    half_a,
    half_b,
    half_c,
    held_a,
    held_b,
    held_c,
    mine_a,
    mine_b,
    mine_c,
    acc_a,
    acc_b,
    acc_c,
    sz,
    rz,
    sx,
    rx,
    sw,
    rw,
    sy,
    ry,
    sb,
    rb,
    s0,
    r0,
    s1,
    r1,
    s2,
    r2,
    s3,
    r3,
    s4,
):
    dp, ch = lax.axis_index("dp"), lax.axis_index("chan")
    x, zh = ch // NH, ch % NH
    core, own = dp % 2, dp // 2
    y, zl = own % NY, own // NY
    xn, xp = (x + 1) % NX, (x + NX - 1) % NX
    yn, yp = (y + 1) % NY, (y + NY - 1) % NY

    def at_chan(x_, z_):
        return (dp, x_ * NH + z_)

    def at_dp(y_, c_):
        return (zl * (2 * NY) + y_ * 2 + c_, ch)

    zdev = [at_chan(x, (zh + k + 1) % NH) for k in range(2)]
    xdev = [at_chan(xn, zh), at_chan(xp, zh)]
    ydev = [at_dp(yn, core), at_dp(yp, core)]
    sib = at_dp(y, 1 - core)

    barrier = pltpu.get_barrier_semaphore()
    for dev in zdev + xdev + [sib]:
        pl.semaphore_signal(barrier, inc=1, device_id=dev, device_id_type=MESH)

    @pl.loop(1, OWN)
    def _(j):
        pl.semaphore_signal(
            barrier, inc=1, device_id=(((own + j) % OWN) * 2 + core, ch), device_id_type=MESH
        )

    lane = iota((TOK, 128), 1)
    pixels = pix[...]
    query = aggq[...].astype(f32)
    score = jnp.zeros((TOK, 128), f32)
    for c in range(CHANNELS):
        masked = jnp.where((lane >= PP * c) & (lane < PP * (c + 1)), pixels, jnp.zeros_like(pixels))
        e = (dot(masked, wemb[...], 1, 0) + bias[c : c + 1, :].astype(f32)).astype(bf16)
        emb[c] = e
        s = jnp.sum(e.astype(f32) * query, 1, keepdims=True)
        score = jnp.where(lane == c, s, score)
    capped = CAP * jnp.tanh(score / CAP)
    agg_exp = jnp.exp(capped) * jnp.where(lane < counts[...], 1.0, 0.0)
    agg_weight = agg_exp / jnp.sum(agg_exp, 1, keepdims=True)
    agg_round = agg_weight.astype(bf16).astype(f32)
    token = jnp.zeros((TOK, D), f32)
    for c in range(CHANNELS):
        token += agg_round[:, c : c + 1] * emb[c].astype(f32)
    tok[...] = token.astype(bf16)
    tok_all[pl.ds(pl.multiple_of(ch * TOK, 32), TOK), :] = tok[...]

    eye = (iota((128, 128), 0) == iota((128, 128), 1)).astype(f32).astype(bf16)
    kq[256 : 256 + HD] = vw[...]
    kq[256 + HD :] = jnp.zeros((HD, D), bf16)
    head_o[:HD] = outw[...]
    head_o[HD:] = jnp.zeros((HD, D), bf16)
    for q in range(4):
        wp[q] = vw[16 * q : 16 * q + 16, :]
        wp[4 + q] = outw[16 * q : 16 * q + 16, :]
    fq8 = jnp.broadcast_to(fq[...].astype(f32), (16, HD)).astype(bf16)
    kt[...] = stacked(dot(fq8, kw[...], 1, 0)[:1])
    kt_all[ch] = kt[...]

    started = []

    def remote(src, dst, ss, rs, dev):
        return pltpu.make_async_remote_copy(
            src_ref=src, dst_ref=dst, send_sem=ss, recv_sem=rs, device_id=dev, device_id_type=MESH
        )

    def send(src, dst, ss, rs, dev):
        copy = remote(src, dst, ss, rs, dev)
        copy.start()
        started.append(copy)

    def arrive(dst, ss, rs):
        remote(dst, dst, ss, rs, sib).wait_recv()

    def owner(dx, k):
        return ((x + NX - dx) % NX) * NH + (zh + NH - k) % NH

    def at_rows(c, start, rows):
        return tok_all.at[pl.ds(pl.multiple_of(c * TOK + start, 16), rows)]

    lanes = pl.multiple_of(core * 512, 512)
    wmine = wp.at[y, :, pl.ds(lanes, 512)]

    def piece(c):
        return w_all.at[pl.ds(pl.multiple_of((y * CH + c) * 16, 16), 16), pl.ds(lanes, 512)]

    small = [(wmine, piece), (kt, lambda c: kt_all.at[c])]

    def part(c, p):
        return at_rows(c, p * PR, PR)

    def half(c, p, h):
        return at_rows(c, p * PR + h * PH, PH)

    place = pltpu.make_async_copy(wmine, piece(ch), s4)
    place.start()
    pl.semaphore_wait(barrier, OWN + 4)

    for i, (src, dst) in enumerate(small):
        for k in range(2):
            send(src, dst(ch), sw.at[i, k], rw.at[i, k], zdev[k])
        for d in range(2):
            send(src, dst(ch), sw.at[i, 2 + 3 * d], rw.at[i, 2 + 3 * d], xdev[d])
    for p in range(PARTS):
        own_part = tok.at[pl.ds(p * PR, PR)]
        for k in range(2):
            send(own_part, part(ch, p), sz.at[k, p], rz.at[k, p], zdev[k])
        for d in range(2):
            send(own_part, part(ch, p), sx.at[d, 0, p], rx.at[d, 0, p], xdev[d])

    place.wait()

    for k in (1, 2):
        for i, (_, dst) in enumerate(small):
            c = owner(0, k)
            arrive(dst(c), sw.at[i, k - 1], rw.at[i, k - 1])
            for d in range(2):
                send(dst(c), dst(c), sw.at[i, 2 + 3 * d + k], rw.at[i, 2 + 3 * d + k], xdev[d])
    for k in range(3):
        for i, (_, dst) in enumerate(small):
            c = owner(1, k)
            arrive(dst(c), sw.at[i, 2 + k], rw.at[i, 2 + k])
            send(dst(c), dst(c), sw.at[i, 8 + k], rw.at[i, 8 + k], xdev[0])

    def relay(k, p):
        c = owner(1, k)
        arrive(part(c, p), sx.at[0, k, p], rx.at[0, k, p])
        send(half(c, p, 0), half(c, p, 0), sx.at[2, k, p], rx.at[2, k, p], xdev[0])
        c = owner(NX - 1, k)
        arrive(part(c, p), sx.at[1, k, p], rx.at[1, k, p])
        send(half(c, p, 1), half(c, p, 1), sx.at[3, k, p], rx.at[3, k, p], xdev[1])

    for p in range(PARTS):
        relay(0, p)
    for k in range(3):
        for i, (_, dst) in enumerate(small):
            c = owner(NX - 1, k)
            arrive(dst(c), sw.at[i, 5 + k], rw.at[i, 5 + k])
            c = owner(2, k)
            arrive(dst(c), sw.at[i, 8 + k], rw.at[i, 8 + k])

    def rows_of(y_, h, core_):
        at = ((y_ + 2 * NY) % NY) * (CH * 16) + h * 96
        return w_all.at[
            pl.ds(pl.multiple_of(at, 32), 96), pl.ds(pl.multiple_of(core_ * 512, 512), 512)
        ]

    def sub(y_, h):
        return rows_of(y_, h, core)

    def ysend(s, h, d):
        block = sub(y - s, h) if d == 0 else sub(y + s, h)
        send(block, block, sy.at[d, s, h], ry.at[d, s, h], ydev[d])

    def yarrive(s):
        for h in range(2):
            for d in range(2):
                if s < 3 or h == d:
                    block = sub(y - 1 - s, h) if d == 0 else sub(y + 1 + s, h)
                    arrive(block, sy.at[d, s, h], ry.at[d, s, h])
                    if s + 1 < 3 or (s + 1 == 3 and h == d):
                        ysend(s + 1, h, d)
                    send(block, block, sb.at[d, s, h], rb.at[d, s, h], sib)

    for h in range(2):
        for d in range(2):
            ysend(0, h, d)
        send(sub(y, h), sub(y, h), sb.at[2, 0, h], rb.at[2, 0, h], sib)
    for p in range(PARTS):
        for k in (1, 2):
            c = owner(0, k)
            arrive(part(c, p), sz.at[k - 1, p], rz.at[k - 1, p])
            for d in range(2):
                send(part(c, p), part(c, p), sx.at[d, k, p], rx.at[d, k, p], xdev[d])
        yarrive(p)
        for k in (1, 2):
            relay(k, p)
    yarrive(3)
    for k in range(3):
        for p in range(PARTS):
            c = owner(2, k)
            arrive(half(c, p, 0), sx.at[2, k, p], rx.at[2, k, p])
            arrive(half(c, p, 1), sx.at[3, k, p], rx.at[3, k, p])
    for h in range(2):
        arrive(rows_of(y, h, 1 - core), sb.at[2, 0, h], rb.at[2, 0, h])
        for s in range(4):
            for d in range(2):
                if s < 3 or h == d:
                    y_ = y - 1 - s if d == 0 else y + 1 + s
                    arrive(rows_of(y_, h, 1 - core), sb.at[d, s, h], rb.at[d, s, h])
    for copy in started:
        copy.wait_send()

    def fold(at):
        return at - 192 * sum((at >= 192 * n).astype(jnp.int32) for n in (1, 2, 3))

    col, row = fold(iota((128, WIDE), 1)), iota((128, WIDE), 0)
    expand = jnp.where((col >= 16 * row) & (col < 16 * row + 16), 1.0, 0.0).astype(bf16)
    row, col = fold(iota((WIDE, 128), 0)), iota((WIDE, 128), 1)
    gather = jnp.where((row >= 16 * col) & (row < 16 * col + 16), 1.0, 0.0).astype(bf16)
    at = iota((128, 128), 0)
    for j in range(8):
        rows = jnp.zeros((128, 128), f32)
        for h in range(HEADS):
            rows = jnp.where(at == h, kt_all[h, j : j + 1, :], rows)
        high, low = split(rows)
        kq[:128, 128 * j : 128 * j + 128] = high
        kq[128:256, 128 * j : 128 * j + 128] = low

    grads = go[...]
    all_grad = dot(grads, w_all[WIDE:, :], 1, 1).astype(bf16).astype(f32)
    my_grad = dot(grads, head_o[...], 1, 1).astype(bf16).astype(f32)

    def rows_at(i):
        return pl.ds(pl.multiple_of(i * ROWS, 128), ROWS)

    def folded(value):
        return jnp.sum(value.reshape(BATCH, TOK, value.shape[1]), 0)

    def tiled(value):
        return jnp.concatenate([value] * BATCH, 0)

    all_tiled = tiled(all_grad)

    def first(i, total):
        t = tok_all[rows_at(i), :]
        v = dot(t, w_all[:WIDE, :], 1, 1).astype(bf16)
        val[rows_at(i), :] = v
        high, low = split(v.astype(f32) * all_tiled)
        pg_s[rows_at(i), :] = dot(high, gather, 1, 0) + dot(low, gather, 1, 0)
        r = dot(t, kq[...], 1, 1)
        th = jnp.tanh((r[:, :128] + r[:, 128:256]) / 8.0 / CAP)
        ex = jnp.exp(CAP * th)
        th_s[rows_at(i), :] = th
        hp_s[rows_at(i), :] = ex
        mv_s[rows_at(i), :] = r[:, 256:].astype(bf16)
        return total + folded(ex)

    total = lax.fori_loop(0, CH // BATCH, first, jnp.zeros((TOK, 128), f32))
    inverse = tiled(1.0 / total)

    def second(i, carry):
        attended, mean = carry
        hp = hp_s[rows_at(i), :] * inverse
        hp_s[rows_at(i), :] = hp
        wide = dot(hp.astype(bf16), expand, 1, 0)
        return (
            attended + folded(wide * val[rows_at(i), :].astype(f32)),
            mean + folded(hp * pg_s[rows_at(i), :]),
        )

    attended, mean = lax.fori_loop(
        0, CH // BATCH, second, (jnp.zeros((TOK, WIDE), f32), jnp.zeros((TOK, 128), f32))
    )
    layer[...] = dot(attended.astype(bf16), w_all[WIDE:, :], 1, 0).astype(bf16)

    lane_tiled = iota((ROWS, 128), 1)
    mine_only = lane_tiled == ch
    mean_tiled, my_tiled = tiled(mean), tiled(my_grad)

    def third(i, my_attended):
        hp, th = hp_s[rows_at(i), :], th_s[rows_at(i), :]
        raw = hp * (pg_s[rows_at(i), :] - mean_tiled) * (1.0 - th * th) / 8.0
        pg_s[rows_at(i), :] = raw
        weight = jnp.sum(
            jnp.where(mine_only, hp.astype(bf16).astype(f32), 0.0), 1, keepdims=True
        )
        high, low = split(jnp.sum(jnp.where(mine_only, raw, 0.0), 1, keepdims=True))
        rows = weight * my_tiled
        rows = jnp.where(lane_tiled == HD, high.astype(f32), rows)
        rows = jnp.where(lane_tiled == HD + 1, low.astype(f32), rows)
        left[rows_at(i), :] = rows.astype(bf16)
        return my_attended + folded(weight * mv_s[rows_at(i), :].astype(f32))

    my_attended = lax.fori_loop(0, CH // BATCH, third, jnp.zeros((TOK, 128), f32))

    def put(ref, i, rows):
        for c in range(2):
            for q in range(2):
                at = 512 * c + 256 * q
                ref[c, 2 * i + q] = rows[:, at : at + 256].astype(bf16)

    def put_small(i, row):
        g_c[i // FEW, i % FEW] = stacked(row).astype(bf16)

    of_tokens = dot(left[...], tok_all[...], 0, 0)
    put_small(9, of_tokens[HD : HD + 1] + of_tokens[HD + 1 : HD + 2])
    of_grads = dot(my_attended.astype(bf16), grads, 0, 0)
    for i in range(8):
        put(g_a, i, of_tokens[8 * i : 8 * i + 8])
        put(g_a, 8 + i, of_grads[8 * i : 8 * i + 8])

    def pair(ref, half, n):
        return remote(ref.at[1 - core], half, s0.at[n], r0.at[n], sib)

    pair(g_a, half_a, 0).start()

    here = pl.ds(pl.multiple_of(ch * TOK, 32), TOK)
    hp, raw = hp_s[here, :], pg_s[here, :]
    wide = dot(hp.astype(bf16), expand, 1, 0)
    high, low = split(raw)
    token_grad = (
        dot((wide * all_grad).astype(bf16), w_all[:WIDE, :], 1, 0)
        + dot(high, kq[:128], 1, 0)
        + dot(high, kq[128:256], 1, 0)
        + dot(low, kq[:128], 1, 0)
    )
    mix = jnp.zeros((TOK, 128), f32)
    for c in range(CHANNELS):
        s = jnp.sum(token_grad * emb[c].astype(f32), 1, keepdims=True)
        mix = jnp.where(lane == c, s, mix)
    agg_raw = (
        agg_weight
        * (mix - jnp.sum(agg_weight * mix, 1, keepdims=True))
        * (1.0 - (capped / CAP) * (capped / CAP))
    )

    def pair_sum(ref, half, acc, n):
        pair(ref, half, n).wait_recv()
        acc[...] = (ref[core].astype(f32) + half[...].astype(f32)).astype(bf16)

    def peer(j):
        return (j * 2 + core, ch)

    def spread_out(acc, held, n):
        @pl.loop(1, OWN)
        def _(j):
            to = (own + j) % OWN
            remote(acc.at[to], held.at[own], s1.at[n, to], r1.at[n, own], peer(to)).start()

    def total_of(acc, held, at, n):
        def add(j, total):
            src = (own + OWN - j) % OWN
            remote(held.at[src], held.at[src], s1.at[n, src], r1.at[n, src], sib).wait_recv()
            return total + held[src].astype(f32)

        return lax.fori_loop(1, OWN, add, acc[at].astype(f32)).astype(bf16)

    def give(mine, out, n):
        @pl.loop(1, OWN)
        def _(j):
            to = (own + j) % OWN
            remote(mine, out.at[core, own], s2.at[n, to], r2.at[n, own], peer(to)).start()

        out[core, own] = mine[...]

    pair_sum(g_a, half_a, acc_a, 0)
    spread_out(acc_a, held_a, 0)

    upright = dot(eye, pixels, 1, 1)
    one = jnp.where(iota((16, TOK), 0) == 0, 1.0, 0.0)
    grad_agg = jnp.zeros((TOK, D), f32)
    for c in range(CHANNELS):
        e = (agg_round[:, c : c + 1] * token_grad + agg_raw[:, c : c + 1] * query).astype(bf16)
        grad_agg += agg_raw[:, c : c + 1] * emb[c].astype(f32)
        rows = jnp.concatenate([upright[PP * c : PP * c + PP], one], 0).astype(bf16)
        res = dot(rows, e, 1, 0)
        put_small(c, res[16:17])
        put(g_b, 2 * c, res[:8])
        put(g_b, 2 * c + 1, res[8:16])
    pair(g_b, half_b, 1).start()
    put_small(8, jnp.sum(grad_agg, 0, keepdims=True))

    pair_sum(g_b, half_b, acc_b, 1)
    pair(g_c, half_c, 2).start()
    spread_out(acc_b, held_b, 1)
    pair_sum(g_c, half_c, acc_c, 2)
    for i in range(FEW):

        @pl.when(own != i)
        def _():
            remote(acc_c.at[i], held_c.at[own], s1.at[2, i], r1.at[2, own], peer(i)).start()

    mine_a[...] = total_of(acc_a, held_a, own, 0)
    give(mine_a, out_a, 0)
    mine_b[...] = total_of(acc_b, held_b, own, 1)
    give(mine_b, out_b, 1)

    @pl.when(own < FEW)
    def _():
        mine_c[...] = total_of(acc_c, held_c, own, 2)
        give(mine_c, out_c, 2)

    def taken(out, n):
        @pl.loop(1, OWN)
        def _(j):
            src = (own + OWN - j) % OWN
            block = out.at[core, src]
            remote(block, block, s2.at[n, src], r2.at[n, src], sib).wait_recv()

    def back(out, n):
        return remote(out.at[core], out.at[core], s3.at[n], r3.at[n], sib)

    taken(out_a, 0)
    back(out_a, 0).start()
    taken(out_b, 1)
    back(out_b, 1).start()
    for i in range(FEW):

        @pl.when(own != i)
        def _():
            block = out_c.at[core, i]
            remote(block, block, s2.at[2, i], r2.at[2, i], sib).wait_recv()

    back(out_c, 2).start()
    for n, out in enumerate((out_a, out_b, out_c)):
        other = out.at[1 - core]
        remote(other, other, s3.at[n], r3.at[n], sib).wait_recv()
        back(out, n).wait_send()
    for n, (ref, half) in enumerate(((g_a, half_a), (g_b, half_b), (g_c, half_c))):
        pair(ref, half, n).wait_send()

    def sent(acc, held, mine, out, n):
        @pl.loop(1, OWN)
        def _(j):
            to = (own + j) % OWN
            remote(acc.at[to], held.at[own], s1.at[n, to], r1.at[n, own], sib).wait_send()
            remote(mine, out.at[core, own], s2.at[n, to], r2.at[n, own], sib).wait_send()

    sent(acc_a, held_a, mine_a, out_a, 0)
    sent(acc_b, held_b, mine_b, out_b, 1)
    for i in range(FEW):

        @pl.when(own != i)
        def _():
            remote(acc_c.at[i], held_c.at[own], s1.at[2, i], r1.at[2, own], sib).wait_send()

    @pl.when(own < FEW)
    def _():
        @pl.loop(1, OWN)
        def _(j):
            to = (own + j) % OWN
            remote(mine_c, out_c.at[core, own], s2.at[2, to], r2.at[2, own], sib).wait_send()


def step(*args):
    vmem = pl.BlockSpec(memory_space=pltpu.VMEM)
    dma = pltpu.SemaphoreType.DMA
    large, few = (OWN, 8, 256), (FEW, 8, 128)
    return pl.pallas_call(
        step_kernel,
        out_shape=(
            jax.ShapeDtypeStruct((TOK, D), bf16),
            jax.ShapeDtypeStruct((2, *large), bf16),
            jax.ShapeDtypeStruct((2, *large), bf16),
            jax.ShapeDtypeStruct((2, *few), bf16),
        ),
        in_specs=[vmem] * len(args),
        out_specs=(vmem,) * 4,
        scratch_shapes=[
            pltpu.VMEM((CHANNELS, TOK, D), bf16),
            pltpu.VMEM((CH * TOK, D), bf16),
            pltpu.VMEM((NY * CH * 16, D), bf16),
            pltpu.VMEM((CH, 8, 128), f32),
            pltpu.VMEM((TOK, D), bf16),
            pltpu.VMEM((NY, 16, D), bf16),
            pltpu.VMEM((8, 128), f32),
            pltpu.VMEM((128, D), bf16),
            pltpu.VMEM((384, D), bf16),
            pltpu.VMEM((CH * TOK, WIDE), bf16),
            pltpu.VMEM((CH * TOK, 128), bf16),
            pltpu.VMEM((CH * TOK, 128), f32),
            pltpu.VMEM((CH * TOK, 128), f32),
            pltpu.VMEM((CH * TOK, 128), f32),
            pltpu.VMEM((CH * TOK, 128), bf16),
            pltpu.VMEM((2, *large), bf16),
            pltpu.VMEM((2, *large), bf16),
            pltpu.VMEM((2, *few), bf16),
            pltpu.VMEM(large, bf16),
            pltpu.VMEM(large, bf16),
            pltpu.VMEM(few, bf16),
            pltpu.VMEM(large, bf16),
            pltpu.VMEM(large, bf16),
            pltpu.VMEM((OWN, 8, 128), bf16),
            pltpu.VMEM(large[1:], bf16),
            pltpu.VMEM(large[1:], bf16),
            pltpu.VMEM(few[1:], bf16),
            pltpu.VMEM(large, bf16),
            pltpu.VMEM(large, bf16),
            pltpu.VMEM(few, bf16),
            dma((2, PARTS)),
            dma((2, PARTS)),
            dma((4, 3, PARTS)),
            dma((4, 3, PARTS)),
            dma((2, 11)),
            dma((2, 11)),
            dma((2, 4, 2)),
            dma((2, 4, 2)),
            dma((3, 4, 2)),
            dma((3, 4, 2)),
            dma((3,)),
            dma((3,)),
            dma((3, OWN)),
            dma((3, OWN)),
            dma((3, OWN)),
            dma((3, OWN)),
            dma((3,)),
            dma((3,)),
            dma,
        ],
        compiler_params=pltpu.CompilerParams(collective_id=0, has_side_effects=True),
        name="step",
    )(*args)


def finish_kernel(layer_in, a, b, few, fq, kw, layer, embed, bias, agg, key, value, query, outg):
    def rows(ref, i):
        parts = [ref[c, 2 * i + q] for c in range(2) for q in range(2)]
        return jnp.concatenate(parts, 1).astype(f32)

    def row(i):
        block = few[i // FEW, i % FEW].astype(f32)
        return jnp.concatenate([block[j : j + 1] for j in range(8)], 1)

    layer[...] = layer_in[...]
    for i in range(16):
        embed[8 * i : 8 * i + 8, :] = rows(b, i)
    for i in range(8):
        bias[i : i + 1, :] = row(i)
        value[8 * i : 8 * i + 8, :] = rows(a, i)
        outg[8 * i : 8 * i + 8, :] = rows(a, 8 + i)
    agg[...] = row(8)
    u_rows = jnp.broadcast_to(row(9), (16, D)).astype(bf16)
    only = jnp.where(iota((16, HD), 0) == 0, fq[...].astype(f32), 0.0).astype(bf16)
    key[...] = dot(only, u_rows, 0, 0)
    query[...] = dot(u_rows, kw[...], 1, 1)[:1]


def finish(*args):
    vmem = pl.BlockSpec(memory_space=pltpu.VMEM)

    def shape(*dims):
        return jax.ShapeDtypeStruct(dims, f32)

    return pl.pallas_call(
        finish_kernel,
        out_shape=(
            jax.ShapeDtypeStruct((TOK, D), bf16),
            shape(CHANNELS * PP, D),
            shape(CHANNELS, D),
            shape(1, D),
            shape(HD, D),
            shape(HD, D),
            shape(1, HD),
            shape(HD, D),
        ),
        in_specs=[vmem] * len(args),
        out_specs=(vmem,) * 8,
        name="finish",
    )(*args)


def per_device(
    pixels,
    embed_weight,
    channel_bias,
    agg_query,
    key_weight,
    value_weight,
    final_query,
    out_weight,
    group_counts,
    grad_output,
):
    key_rows = key_weight.T
    partial = step(
        pixels,
        embed_weight.reshape(CHANNELS * PP, D),
        channel_bias,
        agg_query,
        key_rows,
        value_weight.T,
        final_query,
        out_weight,
        group_counts.reshape(1, 1),
        grad_output,
    )
    layer_out, embed, bias, agg, key, value, query, outg = finish(*partial, final_query, key_rows)
    return layer_out, embed.reshape(CHANNELS, PP, D), bias, agg, key.T, value.T, query, outg


def solution(mesh):
    in_specs = (
        P("dp", "chan"),
        P("chan", None, None),
        P("chan", None),
        P("chan", None),
        P(None, "chan"),
        P(None, "chan"),
        P("chan", None),
        P("chan", None),
        P("chan"),
        P("dp", None),
    )
    out_specs = (
        P("dp", None),
        P("chan", None, None),
        P("chan", None),
        P("chan", None),
        P(None, "chan"),
        P(None, "chan"),
        P("chan", None),
        P("chan", None),
    )
    return jax.shard_map(
        per_device, mesh=mesh, in_specs=in_specs, out_specs=out_specs, check_vma=False
    )
```

```python
import jax
import jax.numpy as jnp
from jax import lax
from jax.experimental import pallas as pl
from jax.experimental.pallas import tpu as pltpu
from jax.sharding import PartitionSpec as P

MESH = pl.DeviceIdType.MESH
NX, NH, NY, NL = 4, 3, 8, 4
CH = NX * NH
TOK, D = 96, 1024
HEADS, HD = 12, 64
WIDE = HEADS * HD
CHANNELS, PP = 8, 16
PARTS = 3
PR = TOK // PARTS
PH = PR // 2
CAP = 15.0
OWN = NY * NL
FEW = 5
ROWS = CH * PR

f32, bf16 = jnp.float32, jnp.bfloat16


def dot(a, b, ca, cb):
    return lax.dot_general(a, b, (((ca,), (cb,)), ((), ())), preferred_element_type=f32)


def iota(shape, dim):
    return lax.broadcasted_iota(jnp.int32, shape, dim)


def split(value):
    high = value.astype(bf16)
    return high, (value - high.astype(f32)).astype(bf16)


def stacked(row):
    at = iota((8, 128), 0)
    out = jnp.zeros((8, 128), f32)
    for j in range(8):
        out = jnp.where(at == j, row[:, 128 * j : 128 * j + 128], out)
    return out


def step_kernel(
    pix_h,
    wemb_h,
    bias_h,
    aggq,
    kw_h,
    vw_h,
    fq,
    outw_h,
    counts,
    go_h,
    layer_h,
    out_a,
    out_b,
    out_c,
    layer,
    pix,
    wemb,
    bias,
    kw,
    vw,
    outw,
    go,
    emb,
    tok_all,
    w_all,
    kt_all,
    tok,
    wp,
    kt,
    head_o,
    kq,
    left,
    th_s,
    hp_s,
    pg_s,
    att_s,
    wide_s,
    g_a,
    g_b,
    g_c,
    half_a,
    half_b,
    half_c,
    held_a,
    held_b,
    held_c,
    mine_a,
    mine_b,
    mine_c,
    acc_a,
    acc_b,
    acc_c,
    sz,
    rz,
    sx,
    rx,
    sw,
    rw,
    sy,
    ry,
    sb,
    rb,
    s0,
    r0,
    s1,
    r1,
    r2,
    s3,
    r3,
    s4,
    s5,
):
    dp, ch = lax.axis_index("dp"), lax.axis_index("chan")
    x, zh = ch // NH, ch % NH
    core, own = dp % 2, dp // 2
    y, zl = own % NY, own // NY
    xn, xp = (x + 1) % NX, (x + NX - 1) % NX
    yn, yp = (y + 1) % NY, (y + NY - 1) % NY

    def at_chan(x_, z_):
        return (dp, x_ * NH + z_)

    def at_dp(y_, c_):
        return (zl * (2 * NY) + y_ * 2 + c_, ch)

    zdev = [at_chan(x, (zh + k + 1) % NH) for k in range(2)]
    xdev = [at_chan(xn, zh), at_chan(xp, zh)]
    ydev = [at_dp(yn, core), at_dp(yp, core)]
    sib = at_dp(y, 1 - core)

    loads = [
        pltpu.make_async_copy(src, dst, s5.at[i])
        for i, (src, dst) in enumerate(
            (
                (vw_h, vw),
                (outw_h, outw),
                (kw_h, kw),
                (pix_h, pix),
                (wemb_h, wemb),
                (bias_h, bias),
                (go_h, go),
            )
        )
    ]
    for copy in loads:
        copy.start()
    barrier = pltpu.get_barrier_semaphore()
    for dev in zdev + xdev + [sib]:
        pl.semaphore_signal(barrier, inc=1, device_id=dev, device_id_type=MESH)

    @pl.loop(1, OWN)
    def _(j):
        pl.semaphore_signal(
            barrier, inc=1, device_id=(((own + j) % OWN) * 2 + core, ch), device_id_type=MESH
        )

    for copy in loads[:3]:
        copy.wait()
    for q in range(4):
        wp[q] = vw[16 * q : 16 * q + 16, :]
        wp[4 + q] = outw[16 * q : 16 * q + 16, :]
    fq8 = jnp.broadcast_to(fq[...].astype(f32), (16, HD)).astype(bf16)
    kt[...] = stacked(dot(fq8, kw[...], 1, 0)[:1])
    kt_all[ch] = kt[...]
    kq[256 : 256 + HD] = vw[...]
    kq[256 + HD :] = jnp.zeros((HD, D), bf16)
    head_o[:HD] = outw[...]
    head_o[HD:] = jnp.zeros((HD, D), bf16)

    started = []

    def remote(src, dst, ss, rs, dev):
        return pltpu.make_async_remote_copy(
            src_ref=src, dst_ref=dst, send_sem=ss, recv_sem=rs, device_id=dev, device_id_type=MESH
        )

    def send(src, dst, ss, rs, dev):
        copy = remote(src, dst, ss, rs, dev)
        copy.start()
        started.append(copy)

    def arrive(dst, ss, rs):
        remote(dst, dst, ss, rs, sib).wait_recv()

    def owner(dx, k):
        return ((x + NX - dx) % NX) * NH + (zh + NH - k) % NH

    def at_rows(c, p, start, rows):
        return tok_all.at[pl.ds(pl.multiple_of(p * ROWS + c * PR + start, 16), rows)]

    lanes = pl.multiple_of(core * 512, 512)
    wmine = wp.at[y, :, pl.ds(lanes, 512)]

    def piece(c):
        at = y * CH + (c % NH) * NX + c // NH
        return w_all.at[pl.ds(pl.multiple_of(at * 16, 16), 16), pl.ds(lanes, 512)]

    small = [(wmine, piece), (kt, lambda c: kt_all.at[c])]

    def part(c, p):
        return at_rows(c, p, 0, PR)

    def half(c, p, h):
        return at_rows(c, p, h * PH, PH)

    pl.semaphore_wait(barrier, OWN + 4)
    place = pltpu.make_async_copy(wmine, piece(ch), s4)
    place.start()

    for i, (src, dst) in enumerate(small):
        for k in range(2):
            send(src, dst(ch), sw.at[i, k], rw.at[i, k], zdev[k])
        for d in range(2):
            send(src, dst(ch), sw.at[i, 2 + 3 * d], rw.at[i, 2 + 3 * d], xdev[d])
    for copy in loads[3:]:
        copy.wait()
    lane = iota((TOK, 128), 1)
    pixels = pix[...]
    query = aggq[...].astype(f32)
    score = jnp.zeros((TOK, 128), f32)
    for c in range(CHANNELS):
        masked = jnp.where((lane >= PP * c) & (lane < PP * (c + 1)), pixels, jnp.zeros_like(pixels))
        e = (dot(masked, wemb[...], 1, 0) + bias[c : c + 1, :].astype(f32)).astype(bf16)
        emb[c] = e
        s = jnp.sum(e.astype(f32) * query, 1, keepdims=True)
        score = jnp.where(lane == c, s, score)
    capped = CAP * jnp.tanh(score / CAP)
    agg_exp = jnp.exp(capped) * jnp.where(lane < counts[...], 1.0, 0.0)
    agg_weight = agg_exp / jnp.sum(agg_exp, 1, keepdims=True)
    agg_round = agg_weight.astype(bf16).astype(f32)
    token = jnp.zeros((TOK, D), f32)
    for c in range(CHANNELS):
        token += agg_round[:, c : c + 1] * emb[c].astype(f32)
    tok[...] = token.astype(bf16)
    for p in range(PARTS):
        tok_all[pl.ds(pl.multiple_of(p * ROWS + ch * PR, 32), PR), :] = tok[p * PR : p * PR + PR, :]

    for p in range(PARTS):
        own_part = tok.at[pl.ds(p * PR, PR)]
        for k in range(2):
            send(own_part, part(ch, p), sz.at[k, p], rz.at[k, p], zdev[k])
        for d in range(2):
            send(own_part, part(ch, p), sx.at[d, 0, p], rx.at[d, 0, p], xdev[d])

    place.wait()

    def relay(k, p):
        c = owner(1, k)
        arrive(part(c, p), sx.at[0, k, p], rx.at[0, k, p])
        send(half(c, p, 0), half(c, p, 0), sx.at[2, k, p], rx.at[2, k, p], xdev[0])
        c = owner(NX - 1, k)
        arrive(part(c, p), sx.at[1, k, p], rx.at[1, k, p])
        send(half(c, p, 1), half(c, p, 1), sx.at[3, k, p], rx.at[3, k, p], xdev[1])

    def small_relay(k):
        for i, (_, dst) in enumerate(small):
            c = owner(1, k)
            arrive(dst(c), sw.at[i, 2 + k], rw.at[i, 2 + k])
            send(dst(c), dst(c), sw.at[i, 8 + k], rw.at[i, 8 + k], xdev[0])

    def small_last(k):
        for i, (_, dst) in enumerate(small):
            c = owner(NX - 1, k)
            arrive(dst(c), sw.at[i, 5 + k], rw.at[i, 5 + k])
            c = owner(2, k)
            arrive(dst(c), sw.at[i, 8 + k], rw.at[i, 8 + k])

    def rows_of(y_, k, core_):
        at = ((y_ + 2 * NY) % NY) * (CH * 16) + ((zh + NH - k) % NH) * (NX * 16)
        return w_all.at[
            pl.ds(pl.multiple_of(at, 64), NX * 16), pl.ds(pl.multiple_of(core_ * 512, 512), 512)
        ]

    def sub(y_, k):
        return rows_of(y_, k, core)

    def goes(s, k, d):
        return s < 3 or (s == 3 and k % 2 == d)

    def ysend(s, k, d):
        block = sub(y - s, k) if d == 0 else sub(y + s, k)
        send(block, block, sy.at[d, s, k], ry.at[d, s, k], ydev[d])

    def ystart(k):
        for d in range(2):
            ysend(0, k, d)
        send(sub(y, k), sub(y, k), sb.at[2, 0, k], rb.at[2, 0, k], sib)

    def yarrive(s):
        for k in range(3):
            for d in range(2):
                if goes(s, k, d):
                    block = sub(y - 1 - s, k) if d == 0 else sub(y + 1 + s, k)
                    arrive(block, sy.at[d, s, k], ry.at[d, s, k])
                    if goes(s + 1, k, d):
                        ysend(s + 1, k, d)
                    send(block, block, sb.at[d, s, k], rb.at[d, s, k], sib)

    small_relay(0)
    for k in (1, 2):
        for i, (_, dst) in enumerate(small):
            c = owner(0, k)
            arrive(dst(c), sw.at[i, k - 1], rw.at[i, k - 1])
            for d in range(2):
                send(dst(c), dst(c), sw.at[i, 2 + 3 * d + k], rw.at[i, 2 + 3 * d + k], xdev[d])
    small_last(0)
    ystart(0)
    for p in range(PARTS):
        relay(0, p)
    for k in (1, 2):
        small_relay(k)
    for k in (1, 2):
        small_last(k)
        ystart(k)

    def load_scores():
        at = iota((128, 128), 0)
        for j in range(8):
            rows = jnp.zeros((128, 128), f32)
            for h in range(HEADS):
                rows = jnp.where(at == h, kt_all[h, j : j + 1, :], rows)
            high, low = split(rows)
            kq[:128, 128 * j : 128 * j + 128] = high
            kq[128:256, 128 * j : 128 * j + 128] = low

    lane_rows = iota((ROWS, 128), 1)
    mine_only = lane_rows == ch

    def folded(value):
        return jnp.sum(value.reshape(CH, PR, value.shape[1]), 0)

    def tiled(value):
        return jnp.concatenate([value] * CH, 0)

    def weight_of(hp):
        return jnp.sum(jnp.where(mine_only, hp.astype(bf16).astype(f32), 0.0), 1, keepdims=True)

    def part_scores(p):
        at, rows = slice(p * ROWS, p * ROWS + ROWS), slice(p * PR, p * PR + PR)
        for k in range(3):
            c = owner(2, k)
            arrive(half(c, p, 0), sx.at[2, k, p], rx.at[2, k, p])
            arrive(half(c, p, 1), sx.at[3, k, p], rx.at[3, k, p])
        r = dot(tok_all[at, :], kq[...], 1, 1)
        th = jnp.tanh((r[:, :128] + r[:, 128:256]) / 8.0 / CAP)
        ex = jnp.exp(CAP * th)
        hp = ex * tiled(1.0 / folded(ex))
        th_s[at, :] = th
        hp_s[at, :] = hp
        att_s[rows, :] = folded(weight_of(hp) * r[:, 256:].astype(bf16).astype(f32))

    for p in range(PARTS):
        for k in (1, 2):
            c = owner(0, k)
            arrive(part(c, p), sz.at[k - 1, p], rz.at[k - 1, p])
            for d in range(2):
                send(part(c, p), part(c, p), sx.at[d, k, p], rx.at[d, k, p], xdev[d])
        yarrive(p)
        if p == PARTS - 1:
            load_scores()
            part_scores(0)
        for k in (1, 2):
            relay(k, p)
    yarrive(3)
    for p in range(1, PARTS):
        part_scores(p)

    def put(ref, i, rows):
        for c in range(2):
            for q in range(2):
                at = 512 * c + 256 * q
                ref[c, 2 * i + q] = rows[:, at : at + 256].astype(bf16)

    def put_small(i, row):
        g_c[i // FEW, i % FEW] = stacked(row).astype(bf16)

    grads = go[...]
    of_grads = dot(att_s[...].astype(bf16), grads, 0, 0)
    for i in range(8):
        put(g_a, 8 + i, of_grads[8 * i : 8 * i + 8])
    my_grad = dot(grads, head_o[...], 1, 1).astype(bf16).astype(f32)

    for k in range(3):
        arrive(rows_of(y, k, 1 - core), sb.at[2, 0, k], rb.at[2, 0, k])
        for s in range(4):
            for d in range(2):
                if goes(s, k, d):
                    y_ = y - 1 - s if d == 0 else y + 1 + s
                    arrive(rows_of(y_, k, 1 - core), sb.at[d, s, k], rb.at[d, s, k])
    for copy in started:
        copy.wait_send()

    def fold(at):
        return at - 192 * sum((at >= 192 * n).astype(jnp.int32) for n in (1, 2, 3))

    def place_of(head):
        return 16 * (4 * head - 11 * sum((head >= 3 * n).astype(jnp.int32) for n in (1, 2, 3)))

    col, row = fold(iota((128, WIDE), 1)), place_of(iota((128, WIDE), 0))
    expand = jnp.where((col >= row) & (col < row + 16), 1.0, 0.0).astype(bf16)
    row, col = fold(iota((WIDE, 128), 0)), place_of(iota((WIDE, 128), 1))
    gather = jnp.where((row >= col) & (row < col + 16), 1.0, 0.0).astype(bf16)

    all_grad = dot(grads, w_all[WIDE:, :], 1, 1).astype(bf16).astype(f32)

    for p in range(PARTS):
        at, rows = slice(p * ROWS, p * ROWS + ROWS), slice(p * PR, p * PR + PR)
        v = dot(tok_all[at, :], w_all[:WIDE, :], 1, 1).astype(bf16).astype(f32)
        high, low = split(v * tiled(all_grad[rows]))
        prob_grad = dot(high, gather, 1, 0) + dot(low, gather, 1, 0)
        hp, th = hp_s[at, :], th_s[at, :]
        wide_s[rows, :] = folded(dot(hp.astype(bf16), expand, 1, 0) * v).astype(bf16)
        raw = hp * (prob_grad - tiled(folded(hp * prob_grad))) * (1.0 - th * th) / 8.0
        pg_s[at, :] = raw
        high, low = split(jnp.sum(jnp.where(mine_only, raw, 0.0), 1, keepdims=True))
        weighted = weight_of(hp) * tiled(my_grad[rows])
        weighted = jnp.where(lane_rows == HD, high.astype(f32), weighted)
        weighted = jnp.where(lane_rows == HD + 1, low.astype(f32), weighted)
        left[at, :] = weighted.astype(bf16)

    of_tokens = dot(left[...], tok_all[...], 0, 0)
    put_small(9, of_tokens[HD : HD + 1] + of_tokens[HD + 1 : HD + 2])
    for i in range(8):
        put(g_a, i, of_tokens[8 * i : 8 * i + 8])

    def pair(ref, half, n):
        return remote(ref.at[1 - core], half, s0.at[n], r0.at[n], sib)

    pair(g_a, half_a, 0).start()

    here = [pl.ds(pl.multiple_of(p * ROWS + ch * PR, 32), PR) for p in range(PARTS)]
    hp = jnp.concatenate([hp_s[at, :] for at in here], 0)
    raw = jnp.concatenate([pg_s[at, :] for at in here], 0)
    wide = dot(hp.astype(bf16), expand, 1, 0)
    high, low = split(raw)
    token_grad = (
        dot((wide * all_grad).astype(bf16), w_all[:WIDE, :], 1, 0)
        + dot(high, kq[:128], 1, 0)
        + dot(high, kq[128:256], 1, 0)
        + dot(low, kq[:128], 1, 0)
    )
    mix = jnp.zeros((TOK, 128), f32)
    for c in range(CHANNELS):
        s = jnp.sum(token_grad * emb[c].astype(f32), 1, keepdims=True)
        mix = jnp.where(lane == c, s, mix)
    agg_raw = (
        agg_weight
        * (mix - jnp.sum(agg_weight * mix, 1, keepdims=True))
        * (1.0 - (capped / CAP) * (capped / CAP))
    )

    def pair_sum(ref, half, acc, n):
        pair(ref, half, n).wait_recv()
        acc[...] = (ref[core].astype(f32) + half[...].astype(f32)).astype(bf16)

    def peer(j):
        return (j * 2 + core, ch)

    def spread_out(acc, held, n):
        @pl.loop(1, OWN)
        def _(j):
            to = (own + j) % OWN
            remote(acc.at[to], held.at[own], s1.at[n, to], r1.at[n, own], peer(to)).start()

    def total_of(acc, held, at, n):
        def add(j, total):
            src = (own + OWN - j) % OWN
            remote(held.at[src], held.at[src], s1.at[n, src], r1.at[n, src], sib).wait_recv()
            return total + held[src].astype(f32)

        return lax.fori_loop(1, OWN, add, acc[at].astype(f32)).astype(bf16)

    def give(mine, out, n):
        @pl.loop(1, OWN)
        def _(j):
            to = (own + j) % OWN
            remote(mine, out.at[core, own], s1.at[n, to], r2.at[n, own], peer(to)).start()

        out[core, own] = mine[...]

    pair_sum(g_a, half_a, acc_a, 0)
    spread_out(acc_a, held_a, 0)

    layer[...] = dot(wide_s[...], w_all[WIDE:, :], 1, 0).astype(bf16)
    store = pltpu.make_async_copy(layer, layer_h, s5.at[7])
    eye = (iota((128, 128), 0) == iota((128, 128), 1)).astype(f32).astype(bf16)
    upright = dot(eye, pixels, 1, 1)
    one = jnp.where(iota((16, TOK), 0) == 0, 1.0, 0.0)
    grad_agg = jnp.zeros((TOK, D), f32)
    for c in range(CHANNELS):
        e = (agg_round[:, c : c + 1] * token_grad + agg_raw[:, c : c + 1] * query).astype(bf16)
        grad_agg += agg_raw[:, c : c + 1] * emb[c].astype(f32)
        rows = jnp.concatenate([upright[PP * c : PP * c + PP], one], 0).astype(bf16)
        res = dot(rows, e, 1, 0)
        put_small(c, res[16:17])
        put(g_b, 2 * c, res[:8])
        put(g_b, 2 * c + 1, res[8:16])
    pair(g_b, half_b, 1).start()
    store.start()
    put_small(8, jnp.sum(grad_agg, 0, keepdims=True))

    pair_sum(g_b, half_b, acc_b, 1)
    pair(g_c, half_c, 2).start()
    spread_out(acc_b, held_b, 1)
    pair_sum(g_c, half_c, acc_c, 2)
    for i in range(FEW):

        @pl.when(own != i)
        def _():
            remote(acc_c.at[i], held_c.at[own], s1.at[2, i], r1.at[2, own], peer(i)).start()

    def spread_sent(acc, held, n):
        @pl.loop(1, OWN)
        def _(j):
            to = (own + j) % OWN
            remote(acc.at[to], held.at[own], s1.at[n, to], r1.at[n, own], sib).wait_send()

    mine_a[...] = total_of(acc_a, held_a, own, 0)
    spread_sent(acc_a, held_a, 0)
    give(mine_a, out_a, 0)
    mine_b[...] = total_of(acc_b, held_b, own, 1)
    spread_sent(acc_b, held_b, 1)
    give(mine_b, out_b, 1)
    for i in range(FEW):

        @pl.when(own != i)
        def _():
            remote(acc_c.at[i], held_c.at[own], s1.at[2, i], r1.at[2, own], sib).wait_send()

    @pl.when(own < FEW)
    def _():
        mine_c[...] = total_of(acc_c, held_c, own, 2)
        give(mine_c, out_c, 2)

    def taken(out, n):
        @pl.loop(1, OWN)
        def _(j):
            src = (own + OWN - j) % OWN
            block = out.at[core, src]
            remote(block, block, s1.at[n, src], r2.at[n, src], sib).wait_recv()

    def back(out, n):
        return remote(out.at[core], out.at[core], s3.at[n], r3.at[n], sib)

    taken(out_a, 0)
    back(out_a, 0).start()
    taken(out_b, 1)
    back(out_b, 1).start()
    for i in range(FEW):

        @pl.when(own != i)
        def _():
            block = out_c.at[core, i]
            remote(block, block, s1.at[2, i], r2.at[2, i], sib).wait_recv()

    back(out_c, 2).start()
    for n, out in enumerate((out_a, out_b, out_c)):
        other = out.at[1 - core]
        remote(other, other, s3.at[n], r3.at[n], sib).wait_recv()
        back(out, n).wait_send()
    for n, (ref, half) in enumerate(((g_a, half_a), (g_b, half_b), (g_c, half_c))):
        pair(ref, half, n).wait_send()

    def given(mine, out, n):
        @pl.loop(1, OWN)
        def _(j):
            to = (own + j) % OWN
            remote(mine, out.at[core, own], s1.at[n, to], r2.at[n, own], sib).wait_send()

    store.wait()
    given(mine_a, out_a, 0)
    given(mine_b, out_b, 1)

    @pl.when(own < FEW)
    def _():
        given(mine_c, out_c, 2)


def step(*args):
    vmem = pl.BlockSpec(memory_space=pltpu.VMEM)
    any_ = pl.BlockSpec(memory_space=pl.ANY)
    dma = pltpu.SemaphoreType.DMA
    large, few = (OWN, 8, 256), (FEW, 8, 128)
    return pl.pallas_call(
        step_kernel,
        out_shape=(
            jax.ShapeDtypeStruct((TOK, D), bf16),
            jax.ShapeDtypeStruct((2, *large), bf16),
            jax.ShapeDtypeStruct((2, *large), bf16),
            jax.ShapeDtypeStruct((2, *few), bf16),
        ),
        in_specs=[any_, any_, any_, vmem, any_, any_, vmem, any_, vmem, any_],
        out_specs=(any_, vmem, vmem, vmem),
        scratch_shapes=[
            pltpu.VMEM((TOK, D), bf16),
            pltpu.VMEM((TOK, CHANNELS * PP), bf16),
            pltpu.VMEM((CHANNELS * PP, D), bf16),
            pltpu.VMEM((CHANNELS, D), bf16),
            pltpu.VMEM((HD, D), bf16),
            pltpu.VMEM((HD, D), bf16),
            pltpu.VMEM((HD, D), bf16),
            pltpu.VMEM((TOK, D), bf16),
            pltpu.VMEM((CHANNELS, TOK, D), bf16),
            pltpu.VMEM((CH * TOK, D), bf16),
            pltpu.VMEM((NY * CH * 16, D), bf16),
            pltpu.VMEM((CH, 8, 128), f32),
            pltpu.VMEM((TOK, D), bf16),
            pltpu.VMEM((NY, 16, D), bf16),
            pltpu.VMEM((8, 128), f32),
            pltpu.VMEM((128, D), bf16),
            pltpu.VMEM((384, D), bf16),
            pltpu.VMEM((CH * TOK, 128), bf16),
            pltpu.VMEM((CH * TOK, 128), f32),
            pltpu.VMEM((CH * TOK, 128), f32),
            pltpu.VMEM((CH * TOK, 128), f32),
            pltpu.VMEM((TOK, 128), f32),
            pltpu.VMEM((TOK, WIDE), bf16),
            pltpu.VMEM((2, *large), bf16),
            pltpu.VMEM((2, *large), bf16),
            pltpu.VMEM((2, *few), bf16),
            pltpu.VMEM(large, bf16),
            pltpu.VMEM(large, bf16),
            pltpu.VMEM(few, bf16),
            pltpu.VMEM(large, bf16),
            pltpu.VMEM(large, bf16),
            pltpu.VMEM((OWN, 8, 128), bf16),
            pltpu.VMEM(large[1:], bf16),
            pltpu.VMEM(large[1:], bf16),
            pltpu.VMEM(few[1:], bf16),
            pltpu.VMEM(large, bf16),
            pltpu.VMEM(large, bf16),
            pltpu.VMEM(few, bf16),
            dma((2, PARTS)),
            dma((2, PARTS)),
            dma((4, 3, PARTS)),
            dma((4, 3, PARTS)),
            dma((2, 11)),
            dma((2, 11)),
            dma((2, 4, 3)),
            dma((2, 4, 3)),
            dma((3, 4, 3)),
            dma((3, 4, 3)),
            dma((3,)),
            dma((3,)),
            dma((3, OWN)),
            dma((3, OWN)),
            dma((3, OWN)),
            dma((3,)),
            dma((3,)),
            dma,
            dma((8,)),
        ],
        compiler_params=pltpu.CompilerParams(collective_id=0, has_side_effects=True),
        name="step",
    )(*args)


def finish_kernel(layer_in, a, b, few, fq, kw, layer, embed, bias, agg, key, value, query, outg):
    def rows(ref, i):
        parts = [ref[c, 2 * i + q] for c in range(2) for q in range(2)]
        return jnp.concatenate(parts, 1).astype(f32)

    def row(i):
        block = few[i // FEW, i % FEW].astype(f32)
        return jnp.concatenate([block[j : j + 1] for j in range(8)], 1)

    layer[...] = layer_in[...]
    for i in range(16):
        embed[8 * i : 8 * i + 8, :] = rows(b, i)
    for i in range(8):
        bias[i : i + 1, :] = row(i)
        value[8 * i : 8 * i + 8, :] = rows(a, i)
        outg[8 * i : 8 * i + 8, :] = rows(a, 8 + i)
    agg[...] = row(8)
    u_rows = jnp.broadcast_to(row(9), (16, D)).astype(bf16)
    only = jnp.where(iota((16, HD), 0) == 0, fq[...].astype(f32), 0.0).astype(bf16)
    key[...] = dot(only, u_rows, 0, 0)
    query[...] = dot(u_rows, kw[...], 1, 1)[:1]


def finish(*args):
    vmem = pl.BlockSpec(memory_space=pltpu.VMEM)

    def shape(*dims):
        return jax.ShapeDtypeStruct(dims, f32)

    return pl.pallas_call(
        finish_kernel,
        out_shape=(
            jax.ShapeDtypeStruct((TOK, D), bf16),
            shape(CHANNELS * PP, D),
            shape(CHANNELS, D),
            shape(1, D),
            shape(HD, D),
            shape(HD, D),
            shape(1, HD),
            shape(HD, D),
        ),
        in_specs=[vmem] * len(args),
        out_specs=(vmem,) * 8,
        name="finish",
    )(*args)


def per_device(
    pixels,
    embed_weight,
    channel_bias,
    agg_query,
    key_weight,
    value_weight,
    final_query,
    out_weight,
    group_counts,
    grad_output,
):
    key_rows = key_weight.T
    partial = step(
        pixels,
        embed_weight.reshape(CHANNELS * PP, D),
        channel_bias,
        agg_query,
        key_rows,
        value_weight.T,
        final_query,
        out_weight,
        group_counts.reshape(1, 1),
        grad_output,
    )
    layer_out, embed, bias, agg, key, value, query, outg = finish(*partial, final_query, key_rows)
    return layer_out, embed.reshape(CHANNELS, PP, D), bias, agg, key.T, value.T, query, outg


def solution(mesh):
    in_specs = (
        P("dp", "chan"),
        P("chan", None, None),
        P("chan", None),
        P("chan", None),
        P(None, "chan"),
        P(None, "chan"),
        P("chan", None),
        P("chan", None),
        P("chan"),
        P("dp", None),
    )
    out_specs = (
        P("dp", None),
        P("chan", None, None),
        P("chan", None),
        P("chan", None),
        P(None, "chan"),
        P(None, "chan"),
        P("chan", None),
        P("chan", None),
    )
    return jax.shard_map(
        per_device, mesh=mesh, in_specs=in_specs, out_specs=out_specs, check_vma=False
    )
```
